256 devices in a mesh: blk: 64 (over x, y_hi, z), sub: 4 (over y_lo, core).
Axes of the slice: x: 4, y: 4 (y_hi: 2, y_lo: 2; y = y_hi * 2 + y_lo), z: 8, core: 2. Of those that a mesh axis runs over, the one named last changes fastest.
Arguments:
- queries: bfloat16 [524288, 512], P(('blk', 'sub')), may hold values from -100 to 100
- keys: bfloat16 [524288, 512], P(('blk', 'sub')), may hold values from -6 to 6
- values: bfloat16 [524288, 512], P(('blk', 'sub')), may hold values from -6 to 6
- global_ids: int32 [2], replicated, may hold values from 0 to 4095
- rand_pick: int32 [4096, 3], P(('blk', 'sub')), may hold values from 0 to 15
Outputs:
- attended: bfloat16 [524288, 512], P(('blk', 'sub'))
The draws below stay inside these ranges and needn't reach their ends.
Inputs may be any that keep to these rules, and one draw needn't show every extreme that they name: `global_ids`: two block numbers below 4096, possibly equal.
All inputs are finite; a program needn't handle non-finite values.
Results may differ from the reference program's by a relative error of at most 0.0047.
Values may be sent and summed in bfloat16 or wider, within the bound.
No kernel may reach another device: no remote copies, remote signals or barrier semaphores. Data moves between devices by JAX's collectives and lax.ppermute only.
A program may use at most 128 MiB of HBM per device.

```python
import math
import jax
import jax.numpy as jnp
from jax import lax

H = 4
DH = 128
BS = 128
QB_DEV = 16
NB = 4096
SEQ = 524288
N_BLK = 64
N_SUB = 4


def base_field(own_key):
    field = jax.random.truncated_normal(jax.random.fold_in(own_key, 3), -6.0, 6.0, (SEQ, H * DH), jnp.float32)
    return field


def draw_queries(key, part):
    field = base_field(jax.random.fold_in(key, 1))
    return field.astype(jnp.bfloat16)


def draw_keys(key, part):
    field = base_field(jax.random.fold_in(key, 2))
    return field.astype(jnp.bfloat16)


def place_ends(values, key, low, largest):
    extent = values.shape
    place = [jax.random.randint(jax.random.fold_in(key, axis), (), 0, extent[axis]) for axis in range(len(extent))]
    values = values.at[tuple(place)].set(low)
    longest = extent.index(max(extent))
    place[longest] = (place[longest] + 1) % extent[longest]
    return values.at[tuple(place)].set(largest)


def block_scale(key, extent, split, smallest, top_value):
    level, own = 1.0, jax.random.fold_in(key, 6)
    for axis_at, shards_of in split:
        steps = jnp.exp(jax.random.uniform(jax.random.fold_in(own, axis_at), (shards_of,), jnp.float32, smallest / len(split), top_value / len(split)))
        level = level * jnp.repeat(steps, extent[axis_at] // shards_of).reshape([-1 if axis == axis_at else 1 for axis in range(len(extent))])
    return level


def noise(key, dims, width, bound, shards=(), held_as=jnp.bfloat16):
    drawn = jax.random.normal(key, dims, jnp.float32) * width
    if len(shards) > 0:
        drawn = block_scale(key, dims, shards, -0.22, 0.18) * drawn
    return jnp.clip(drawn, min=-bound, max=bound).astype(held_as)


def setup_inputs(seed: int = 0) -> dict:
    streams_of = jax.random.split(jax.random.key(seed), 6)
    queries = draw_queries(jax.random.fold_in(streams_of[5], 71), 0)
    keys = draw_keys(jax.random.fold_in(streams_of[5], 71), 0)
    values = noise(streams_of[2], (SEQ, H * DH), 1.0, 6.0, ((0, 256),))
    global_ids = jax.random.randint(streams_of[3], (2,), 0, NB).astype(jnp.int32)
    rand_pick = place_ends(jax.random.randint(streams_of[4], (NB, 3), 0, QB_DEV), jax.random.fold_in(streams_of[4], 1), 0, QB_DEV - 1).astype(jnp.int32)
    return {"queries": queries, "keys": keys, "values": values, "global_ids": global_ids, "rand_pick": rand_pick}


def attend(query_rows, key_rows, value_rows):
    group_count = query_rows.shape[0]
    score_scale = 1.0 / math.sqrt(DH)
    query_heads = query_rows.reshape(group_count, BS, H, DH).astype(jnp.float32)
    key_heads = key_rows.reshape(group_count, -1, H, DH).astype(jnp.float32)
    value_heads = value_rows.reshape(group_count, -1, H, DH).astype(jnp.float32)
    scores = jnp.einsum('gqhd,gkhd->ghqk', query_heads, key_heads) * score_scale
    row_max = lax.optimization_barrier(jnp.max(scores, axis=-1, keepdims=True))
    weights = jnp.exp(scores - row_max)
    totals = lax.optimization_barrier(jnp.sum(weights, axis=-1))
    rounded = lax.optimization_barrier(weights.astype(jnp.bfloat16)).astype(jnp.float32)
    mixed = jnp.einsum('ghqk,gkhd->gqhd', rounded, value_heads)
    mixed = mixed / jnp.transpose(totals, (0, 2, 1))[..., None]
    return mixed.astype(jnp.bfloat16).reshape(group_count, BS, H * DH)

def reference(queries, keys, values, global_ids, rand_pick):
    index = jnp.arange(NB, dtype=jnp.int32)
    device = index // QB_DEV
    outer = device // N_SUB
    inner = device % N_SUB
    columns = [(index - 1) % NB, index, (index + 1) % NB]
    columns.append(jnp.zeros((NB,), jnp.int32) + global_ids[0])
    columns.append(jnp.zeros((NB,), jnp.int32) + global_ids[1])
    distances = [N_BLK // 4, N_BLK // 2, 3 * N_BLK // 4]
    for which_random in range(3):
        source = (outer + distances[which_random]) % N_BLK * N_SUB + inner
        columns.append(source * QB_DEV + rand_pick[:, which_random])
    table = jnp.stack(columns, axis=1).astype(jnp.int32)
    feature_width = H * DH
    query_blocks = queries.reshape(NB, BS, feature_width)
    key_blocks = keys.reshape(NB, BS, feature_width)
    value_blocks = values.reshape(NB, BS, feature_width)

    def one_group(group_index):
        first_block = group_index * 4
        chosen = lax.dynamic_slice_in_dim(table, first_block, 4, 0)
        key_rows = jnp.take(key_blocks, chosen, axis=0).reshape(4, 8 * BS, feature_width)
        value_rows = jnp.take(value_blocks, chosen, axis=0).reshape(4, 8 * BS, feature_width)
        query_rows = lax.dynamic_slice_in_dim(query_blocks, first_block, 4, 0)
        return attend(query_rows, key_rows, value_rows)
    result = lax.map(one_group, jnp.arange(NB // 4, dtype=jnp.int32))
    return result.reshape(SEQ, feature_width)
```

```python
import functools
import math

import jax
import jax.numpy as jnp
from jax import lax
from jax.experimental import pallas as pl
from jax.experimental.pallas import tpu as pltpu
from jax.sharding import PartitionSpec as P

H = 4
DH = 128
BS = 128
W = H * DH
SCALE_LOG2 = math.log2(math.e) / math.sqrt(DH)
G_N, A_N, B_N = 2, 6, 8
ANY = pl.BlockSpec(memory_space=pl.ANY)
VM = pl.BlockSpec(memory_space=pltpu.VMEM)
SM = pl.BlockSpec(memory_space=pltpu.SMEM)


def first_two(gids, blocks):
    p0 = lax.rem(gids[0], blocks)
    p1 = lax.rem(gids[1], blocks)
    p1 = jnp.where(p1 == p0, lax.rem(p0 + 1, blocks), p1)
    return p0, p1, jnp.minimum(p0, p1), jnp.maximum(p0, p1)


def block_at(position, places):
    p0, p1, low, high = places
    if position == 0:
        return p0
    if position == 1:
        return p1
    k = position - 2
    k = k + (k >= low).astype(jnp.int32)
    return k + (k >= high).astype(jnp.int32)


def position_of(block, places):
    p0, p1, low, high = places
    rest = block - (block > low).astype(jnp.int32) - (block > high).astype(jnp.int32) + 2
    return jnp.where(block == p0, 0, jnp.where(block == p1, 1, rest))


def pack_kernel(start, count, gids, keys, values, out, buf, in_sem, out_sem):
    places = first_two(gids, keys.shape[0])
    loads = []
    for i in range(count):
        block = block_at(start + i, places)
        pair = []
        for half, ref in enumerate((keys, values)):
            copy = pltpu.make_async_copy(ref.at[block], buf.at[i, half], in_sem.at[i, half])
            copy.start()
            pair.append(copy)
        loads.append(pair)
    stores = []
    for i in range(count):
        for copy in loads[i]:
            copy.wait()
        copy = pltpu.make_async_copy(buf.at[i], out.at[i], out_sem.at[i])
        copy.start()
        stores.append(copy)
    for copy in stores:
        copy.wait()


def pack(gids, keys, values, start, count):
    return pl.pallas_call(
        functools.partial(pack_kernel, start, count),
        out_shape=jax.ShapeDtypeStruct((count, 2, BS, W), keys.dtype),
        in_specs=[SM, ANY, ANY],
        out_specs=ANY,
        scratch_shapes=[
            pltpu.VMEM((count, 2, BS, W), keys.dtype),
            pltpu.SemaphoreType.DMA((count, 2)),
            pltpu.SemaphoreType.DMA((count,)),
        ],
        cost_estimate=pl.CostEstimate(
            flops=0, transcendentals=0, bytes_accessed=count * 4 * BS * W * 2
        ),
        name="pack",
    )(gids, keys, values)


def dot_t(a, b):
    return lax.dot_general(a, b, (((1,), (1,)), ((), ())), preferred_element_type=jnp.float32)


def dot(a, b):
    return lax.dot_general(a, b, (((1,), (0,)), ((), ())), preferred_element_type=jnp.float32)


def attend_parts(q, key_parts, value_parts, old):
    scores = [dot_t(q, k) * SCALE_LOG2 for k in key_parts]
    top = functools.reduce(jnp.maximum, [jnp.max(s, axis=1, keepdims=True) for s in scores])
    if old is not None:
        top = jnp.maximum(top, old[0])
    weights = [jnp.exp2(s - top) for s in scores]
    total = functools.reduce(jnp.add, [jnp.sum(w, axis=1, keepdims=True) for w in weights])
    mixed = functools.reduce(
        jnp.add, [dot(w.astype(jnp.bfloat16), v) for w, v in zip(weights, value_parts)]
    )
    if old is not None:
        fade = jnp.exp2(old[0] - top)
        total = total + fade * old[1]
        mixed = mixed + fade * old[2]
    return top, total, mixed


def put_stats(stats_ref, j, tops, totals):
    lane = lax.broadcasted_iota(jnp.int32, (BS, 128), 1)
    packed = jnp.zeros((BS, 128), jnp.float32)
    for h in range(H):
        packed = jnp.where(lane == h, tops[h], packed)
        packed = jnp.where(lane == H + h, totals[h], packed)
    stats_ref[j] = packed


def head(h):
    return slice(h * DH, (h + 1) * DH)


def window_kernel(blocks, q_ref, keys, values, low, high, stats_ref, acc_ref, kbuf, vbuf, sem):
    copies = []
    for half, (ref, buf) in enumerate(((keys, kbuf), (values, vbuf))):
        copies.append(pltpu.make_async_copy(ref, buf.at[pl.ds(BS, blocks * BS)], sem.at[half, 0]))
        copies.append(pltpu.make_async_copy(low.at[half], buf.at[pl.ds(0, BS)], sem.at[half, 1]))
        copies.append(
            pltpu.make_async_copy(high.at[half], buf.at[pl.ds((blocks + 1) * BS, BS)], sem.at[half, 2])
        )
    for copy in copies:
        copy.start()
    for copy in copies:
        copy.wait()

    def step(j, carry):
        rows = pl.ds(pl.multiple_of(j * BS, BS), BS)
        span = pl.ds(pl.multiple_of(j * BS, BS), 3 * BS)
        tops, totals = [], []
        for h in range(H):
            top, total, mixed = attend_parts(
                q_ref[rows, head(h)], [kbuf[span, head(h)]], [vbuf[span, head(h)]], None
            )
            tops.append(top)
            totals.append(total)
            acc_ref[rows, head(h)] = mixed
        put_stats(stats_ref, j, tops, totals)
        return carry

    lax.fori_loop(0, blocks, step, 0)


def window(queries, keys, values, low, high):
    rows = queries.shape[0]
    blocks = rows // BS
    return pl.pallas_call(
        functools.partial(window_kernel, blocks),
        out_shape=(
            jax.ShapeDtypeStruct((blocks, BS, 128), jnp.float32),
            jax.ShapeDtypeStruct((rows, W), jnp.float32),
        ),
        in_specs=[VM, ANY, ANY, ANY, ANY],
        out_specs=(VM, VM),
        scratch_shapes=[
            pltpu.VMEM(((blocks + 2) * BS, W), keys.dtype),
            pltpu.VMEM(((blocks + 2) * BS, W), keys.dtype),
            pltpu.SemaphoreType.DMA((2, 3)),
        ],
        compiler_params=pltpu.CompilerParams(vmem_limit_bytes=40 << 20),
        cost_estimate=pl.CostEstimate(
            flops=rows * 3 * BS * W * 4, transcendentals=rows * 3 * BS * H, bytes_accessed=12 << 20
        ),
        name="window",
    )(queries, keys, values, low, high)


def near_kernel(
    blocks, gids, picks, q_ref, g_r, a_r, b_r, g_l, a_l, b_l, shared, stats_in, acc_in,
    stats_ref, acc_ref, buf, sem,
):
    copies = []
    for side, parts in enumerate(((g_r, a_r, b_r), (g_l, a_l, b_l))):
        at = 0
        for n, part in enumerate(parts):
            copies.append(
                pltpu.make_async_copy(part, buf.at[side, pl.ds(at, part.shape[0])], sem.at[side, n])
            )
            at += part.shape[0]
    for copy in copies:
        copy.start()
    for copy in copies:
        copy.wait()
    places = first_two(gids, blocks)

    def step(j, carry):
        rows = pl.ds(pl.multiple_of(j * BS, BS), BS)
        near = position_of(picks[j, 0], places)
        far = position_of(picks[j, 2], places)
        stats = stats_in[j]
        tops, totals = [], []
        for h in range(H):
            c = head(h)
            key_parts = [buf[0, near, 0, :, c], buf[1, far, 0, :, c], shared[0, 0, :, c], shared[1, 0, :, c]]
            value_parts = [buf[0, near, 1, :, c], buf[1, far, 1, :, c], shared[0, 1, :, c], shared[1, 1, :, c]]
            old = (stats[:, h : h + 1], stats[:, H + h : H + h + 1], acc_in[rows, c])
            top, total, mixed = attend_parts(q_ref[rows, c], key_parts, value_parts, old)
            tops.append(top)
            totals.append(total)
            acc_ref[rows, c] = mixed
        put_stats(stats_ref, j, tops, totals)
        return carry

    lax.fori_loop(0, blocks, step, 0)


def near(gids, picks, queries, from_right, from_left, shared, stats, acc):
    rows = queries.shape[0]
    blocks = rows // BS
    return pl.pallas_call(
        functools.partial(near_kernel, blocks),
        out_shape=(
            jax.ShapeDtypeStruct(stats.shape, jnp.float32),
            jax.ShapeDtypeStruct(acc.shape, jnp.float32),
        ),
        in_specs=[SM, SM, VM] + [ANY] * 6 + [VM, VM, VM],
        out_specs=(VM, VM),
        scratch_shapes=[
            pltpu.VMEM((2, blocks, 2, BS, W), queries.dtype),
            pltpu.SemaphoreType.DMA((2, 3)),
        ],
        compiler_params=pltpu.CompilerParams(vmem_limit_bytes=40 << 20),
        cost_estimate=pl.CostEstimate(
            flops=rows * 4 * BS * W * 4, transcendentals=rows * 4 * BS * H, bytes_accessed=20 << 20
        ),
        name="near",
    )(gids, picks, queries, *from_right, *from_left, shared, stats, acc)


def last_kernel(
    blocks, gids, picks, queries, g_o, a_o, b_o, stats, acc, out,
    qbuf, kvbuf, sbuf, abuf, obuf, kv_sem, in_sem, out_sem,
):
    places = first_two(gids, blocks)

    def pieces(j):
        rows = pl.ds(pl.multiple_of(j * BS, BS), BS)
        return (
            pltpu.make_async_copy(queries.at[rows], qbuf.at[j], in_sem.at[j, 0]),
            pltpu.make_async_copy(stats.at[j], sbuf.at[j], in_sem.at[j, 1]),
            pltpu.make_async_copy(acc.at[rows], abuf.at[j], in_sem.at[j, 2]),
        )

    def fetch(j, carry):
        position = position_of(picks[j, 1], places)

        @pl.when(position < G_N)
        def _():
            pltpu.make_async_copy(g_o.at[jnp.minimum(position, G_N - 1)], kvbuf.at[j], kv_sem.at[j]).start()

        @pl.when((position >= G_N) & (position < G_N + A_N))
        def _():
            at = jnp.clip(position - G_N, 0, A_N - 1)
            pltpu.make_async_copy(a_o.at[at], kvbuf.at[j], kv_sem.at[j]).start()

        @pl.when(position >= G_N + A_N)
        def _():
            at = jnp.clip(position - G_N - A_N, 0, B_N - 1)
            pltpu.make_async_copy(b_o.at[at], kvbuf.at[j], kv_sem.at[j]).start()

        for copy in pieces(j):
            copy.start()
        return carry

    lax.fori_loop(0, blocks, fetch, 0)

    def store(j):
        rows = pl.ds(pl.multiple_of(j * BS, BS), BS)
        return pltpu.make_async_copy(obuf.at[j], out.at[rows], out_sem.at[j])

    def step(j, carry):
        pltpu.make_async_copy(b_o.at[0], kvbuf.at[j], kv_sem.at[j]).wait()
        for copy in pieces(j):
            copy.wait()
        s = sbuf[j]
        for h in range(H):
            c = head(h)
            old = (s[:, h : h + 1], s[:, H + h : H + h + 1], abuf[j, :, c])
            _, total, mixed = attend_parts(qbuf[j, :, c], [kvbuf[j, 0, :, c]], [kvbuf[j, 1, :, c]], old)
            obuf[j, :, c] = (mixed / total).astype(obuf.dtype)
        store(j).start()
        return carry

    lax.fori_loop(0, blocks, step, 0)

    def drain(j, carry):
        store(j).wait()
        return carry

    lax.fori_loop(0, blocks, drain, 0)


def last(gids, picks, queries, opposite, stats, acc):
    rows = queries.shape[0]
    blocks = rows // BS
    return pl.pallas_call(
        functools.partial(last_kernel, blocks),
        out_shape=jax.ShapeDtypeStruct(queries.shape, queries.dtype),
        in_specs=[SM, SM] + [ANY] * 6,
        out_specs=ANY,
        scratch_shapes=[
            pltpu.VMEM((blocks, BS, W), queries.dtype),
            pltpu.VMEM((blocks, 2, BS, W), queries.dtype),
            pltpu.VMEM((blocks, BS, 128), jnp.float32),
            pltpu.VMEM((blocks, BS, W), jnp.float32),
            pltpu.VMEM((blocks, BS, W), queries.dtype),
            pltpu.SemaphoreType.DMA((blocks,)),
            pltpu.SemaphoreType.DMA((blocks, 3)),
            pltpu.SemaphoreType.DMA((blocks,)),
        ],
        compiler_params=pltpu.CompilerParams(vmem_limit_bytes=40 << 20),
        cost_estimate=pl.CostEstimate(
            flops=rows * BS * W * 4, transcendentals=rows * BS * H, bytes_accessed=14 << 20
        ),
        name="last",
    )(gids, picks, queries, *opposite, stats, acc)


ALL = ("blk", "sub")


def swap_bit(value, bit):
    count = lax.axis_size(ALL)
    return lax.ppermute(value, ALL, [(i, i ^ (1 << bit)) for i in range(count)])


def pick_slots(mask, a, b):
    return jnp.where(mask[:, None, None], a, b)


def spread(start, me, owners):
    def same(bit):
        return ((me >> bit) & 1) == ((owners >> bit) & 1)

    value = start
    for bit in (0, 1):
        half = value.shape[1] // 2
        mine = (me >> bit) & 1
        keep = lax.dynamic_slice_in_dim(value, mine * half, half, 1)
        give = lax.dynamic_slice_in_dim(value, (1 - mine) * half, half, 1)
        value = pick_slots(same(bit), keep, swap_bit(give, bit))
    for bit in (2, 3, 4, 5):
        value = pick_slots(same(bit), value, swap_bit(value, bit))
    for bit in (1, 0):
        other = swap_bit(value, bit)
        first = ((me >> bit) & 1) == 0
        value = jnp.concatenate(
            [jnp.where(first, value, other), jnp.where(first, other, value)], axis=1
        )
    return value


def per_device(queries, keys, values, global_ids, rand_pick):
    rows, width = queries.shape
    blocks = rows // BS
    count = lax.axis_size("blk")
    quarter = count // 4
    right = [(i, (i + quarter) % count) for i in range(count)]
    left = [(i, (i - quarter) % count) for i in range(count)]
    to_right = lambda v: lax.ppermute(v, "blk", right)
    to_left = lambda v: lax.ppermute(v, "blk", left)
    everyone = lax.axis_size(ALL)
    forward = [(i, (i + 1) % everyone) for i in range(everyone)]
    backward = [(i, (i - 1) % everyone) for i in range(everyone)]

    key_blocks = keys.reshape(blocks, BS, width)
    value_blocks = values.reshape(blocks, BS, width)
    g = pack(global_ids, key_blocks, value_blocks, 0, G_N)
    g_l, g_r = to_right(g), to_left(g)
    a = pack(global_ids, key_blocks, value_blocks, G_N, A_N)
    b = pack(global_ids, key_blocks, value_blocks, G_N + A_N, B_N)
    a_l, b_r = to_right(a), to_left(b)
    low = lax.ppermute(jnp.stack([key_blocks[-1], value_blocks[-1]]), ALL, forward)
    high = lax.ppermute(jnp.stack([key_blocks[0], value_blocks[0]]), ALL, backward)

    g_o = to_right(g_l)
    b_l, a_r = to_right(b), to_left(a)
    stats, acc = window(queries, keys, values, low, high)
    a_o = to_right(a_l)
    b_o = to_left(b_r)

    me = lax.axis_index(ALL)
    owners = global_ids // blocks
    plane = everyone // 4
    distance = lax.rem(owners // plane - me // plane + 4, 4)
    slots = jnp.stack(
        [jnp.zeros((), jnp.int32), (lax.rem(global_ids[1], blocks) != lax.rem(global_ids[0], blocks)).astype(jnp.int32)]
    )

    def slotted(v):
        v = v.reshape(G_N, 2 * BS, width)
        return jnp.where((slots == 0)[:, None, None], v[0][None], v)

    start = slotted(g)
    for d, v in ((1, g_r), (2, g_o), (3, g_l)):
        start = pick_slots(distance == d, slotted(v), start)
    shared = spread(start, me, owners).reshape(2, 2, BS, width)

    stats, acc = near(
        global_ids, rand_pick, queries, (g_r, a_r, b_r), (g_l, a_l, b_l), shared, stats, acc
    )
    return last(global_ids, rand_pick, queries, (g_o, a_o, b_o), stats, acc)


def solution(mesh):
    return jax.shard_map(
        per_device,
        mesh=mesh,
        in_specs=(
            P(("blk", "sub"), None),
            P(("blk", "sub"), None),
            P(("blk", "sub"), None),
            P(),
            P(("blk", "sub"), None),
        ),
        out_specs=P(("blk", "sub"), None),
        check_vma=False,
    )
```

```python
import functools
import math

import jax
import jax.numpy as jnp
from jax import lax
from jax.experimental import pallas as pl
from jax.experimental.pallas import tpu as pltpu
from jax.sharding import PartitionSpec as P


H = 4
DH = 128
BS = 128
QB = 16
GROUP = 4
W = H * DH
SCALE_LOG2 = math.log2(math.e) / math.sqrt(DH)
G_N, A_N, B_N = 2, 6, 8
NEAR_VMEM, SCORE_VMEM, LAST_VMEM = 24 << 20, 24 << 20, 12 << 20
ANY = pl.BlockSpec(memory_space=pl.ANY)
VM = pl.BlockSpec(memory_space=pltpu.VMEM)
SM = pl.BlockSpec(memory_space=pltpu.SMEM)
HB = pl.BlockSpec(memory_space=pltpu.HBM)


def first_two(gids, blocks):
    p0 = blocks - 1 - lax.rem(gids[0], blocks)
    p1 = blocks - 1 - lax.rem(gids[1], blocks)
    p1 = jnp.where(p1 == p0, lax.rem(p0 + 1, blocks), p1)
    return p0, p1, jnp.minimum(p0, p1), jnp.maximum(p0, p1)


def block_at(position, places, blocks):
    p0, p1, low, high = places
    if position == 0:
        return blocks - 1 - p0
    if position == 1:
        return blocks - 1 - p1
    k = position - 2
    k = k + (k >= low).astype(jnp.int32)
    return blocks - 1 - (k + (k >= high).astype(jnp.int32))


def position_of(block, places, blocks):
    p0, p1, low, high = places
    label = blocks - 1 - block
    rest = label - (label > low).astype(jnp.int32) - (label > high).astype(jnp.int32) + 2
    return jnp.where(label == p0, 0, jnp.where(label == p1, 1, rest))


def pack_kernel(start, count, joined, ends, gids, keys, values, *refs):
    blocks = keys.shape[0]
    places = first_two(gids, blocks)
    outs, (buf, in_sem, out_sem) = refs[:-3], refs[-3:]
    if joined:
        buf = outs[0]
    wanted = [block_at(start + i, places, blocks) for i in range(count)]
    if ends:
        wanted += [blocks - 1, 0]
    loads, stores = [], []
    for half, ref in enumerate((keys, values)):
        for i, block in enumerate(wanted):
            copy = pltpu.make_async_copy(ref.at[block], buf.at[half, i], in_sem.at[half, i])
            copy.start()
            loads.append((half, i, copy))
    for half, i, load in loads:
        load.wait()
        if joined:
            continue
        target = outs[half].at[i] if i < count else outs[2 + i - count].at[half]
        copy = pltpu.make_async_copy(buf.at[half, i], target, out_sem.at[half, i])
        copy.start()
        stores.append(copy)
    for copy in stores:
        copy.wait()


def pack(gids, keys, values, start, count, joined=False, ends=False):
    shapes = [jax.ShapeDtypeStruct((count, BS, W), keys.dtype)] * 2
    if joined:
        shapes = [jax.ShapeDtypeStruct((2, count, BS, W), keys.dtype)]
    if ends:
        shapes += [jax.ShapeDtypeStruct((2, BS, W), keys.dtype)] * 2
    places = count + 2 * ends
    return pl.pallas_call(
        functools.partial(pack_kernel, start, count, joined, ends),
        out_shape=shapes,
        in_specs=[SM, HB, HB],
        out_specs=[VM if joined else ANY] * len(shapes),
        scratch_shapes=[
            pltpu.VMEM((2, 1 if joined else places, BS, W), keys.dtype),
            pltpu.SemaphoreType.DMA((2, places)),
            pltpu.SemaphoreType.DMA((2, places)),
        ],
        compiler_params=pltpu.CompilerParams(vmem_limit_bytes=56 << 20),
        cost_estimate=pl.CostEstimate(
            flops=0, transcendentals=0, bytes_accessed=places * 4 * BS * W * 2
        ),
        name="pack",
    )(gids, keys, values)


def dot_t(a, b):
    return lax.dot_general(a, b, (((1,), (1,)), ((), ())), preferred_element_type=jnp.float32)


def dot(a, b):
    return lax.dot_general(a, b, (((1,), (0,)), ((), ())), preferred_element_type=jnp.float32)


def head(h):
    return slice(h * DH, (h + 1) * DH)


def wide(column):
    return jnp.broadcast_to(column, (BS, DH))


def ones(rows):
    return jnp.ones((rows, DH), jnp.bfloat16)


def top_of(scores, old=None):
    tops = [jnp.max(s, axis=1, keepdims=True) for s in scores]
    top = wide(functools.reduce(jnp.maximum, tops))
    return top if old is None else jnp.maximum(top, old)


def weigh(s, top):
    parts = [
        jnp.exp2((s[:, n : n + DH] - top) * SCALE_LOG2) for n in range(0, s.shape[1], DH)
    ]
    return jnp.concatenate(parts, axis=1).astype(jnp.bfloat16)


def mix(w, v):
    return dot(w, jnp.concatenate([v, ones(v.shape[0])], axis=1))


def state_of(blocks):
    return [jax.ShapeDtypeStruct((blocks, H, BS, DH), jnp.float32)] * 3


def fetch_pick(position, parts, dst, sem):
    at = 0
    for part in parts:
        count = part.shape[0]

        @pl.when((position >= at) & (position < at + count))
        def _(part=part, at=at, count=count):
            pltpu.make_async_copy(part.at[jnp.clip(position - at, 0, count - 1)], dst, sem).start()

        at += count


def near_kernel(blocks, gids, picks, place, q_ref, keys, values, low, high, first, last, *refs):
    side, refs = refs[:5], refs[5:]
    pieces, refs = refs[:4], refs[4:]
    top_ref, total_ref, acc_ref, kbuf, vbuf, shared, buf, sem, shared_sem, pick_sem = refs
    places = first_two(gids, blocks)
    copies = []
    for half, (ref, dst) in enumerate(((keys, kbuf), (values, vbuf))):
        copies.append(pltpu.make_async_copy(ref, dst.at[pl.ds(BS, blocks * BS)], sem.at[half, 0]))
    for n, piece in enumerate(pieces):
        quarter = jnp.bitwise_and(jnp.bitwise_xor(place[0], n), 3)
        rows = piece.shape[1]
        start = jnp.bitwise_and(quarter, 1) * (2 * rows) + jnp.right_shift(quarter, 1) * rows
        at = pl.ds(pl.multiple_of(start, rows), rows)
        copies.append(pltpu.make_async_copy(piece, shared.at[:, at], shared_sem.at[n]))
    for copy in copies:
        copy.start()

    halos = (
        (1, place[3] == 0, first, low, 0),
        (2, place[3] == 1, last, high, (blocks + 1) * BS),
    )
    for n, wraps, there, here, at in halos:
        for half, dst in enumerate((kbuf, vbuf)):

            @pl.when(wraps)
            def _(there=there, half=half, dst=dst, at=at, n=n):
                pltpu.make_async_copy(there.at[half], dst.at[pl.ds(at, BS)], sem.at[half, n]).start()

            @pl.when(jnp.logical_not(wraps))
            def _(here=here, half=half, dst=dst, at=at, n=n):
                pltpu.make_async_copy(here.at[half], dst.at[pl.ds(at, BS)], sem.at[half, n]).start()

    g, a_k, b_k, a_v, b_v = side

    def fetch(j, carry):
        position = position_of(picks[j, 0], places, blocks)
        fetch_pick(position, (g.at[0], a_k, b_k), buf.at[j, 0], pick_sem.at[j, 0])
        fetch_pick(position, (g.at[1], a_v, b_v), buf.at[j, 1], pick_sem.at[j, 1])
        return carry

    lax.fori_loop(0, blocks, fetch, 0)
    for copy in copies:
        copy.wait()
    for n, _, _, here, at in halos:
        for half, dst in enumerate((kbuf, vbuf)):
            pltpu.make_async_copy(here.at[half], dst.at[pl.ds(at, BS)], sem.at[half, n]).wait()

    def step(j, carry):
        rows = pl.ds(pl.multiple_of(j * BS, BS), BS)
        span = pl.ds(pl.multiple_of(j * BS, BS), 3 * BS)
        for half in range(2):
            pltpu.make_async_copy(b_k.at[0], buf.at[j, half], pick_sem.at[j, half]).wait()
        for first in range(0, H, GROUP):
            heads = range(first, first + GROUP)
            keys_of, values_of = [
                [
                    jnp.concatenate(
                        [
                            own[span, head(h)],
                            buf[j, half, :, head(h)],
                            shared[0, half * BS : (half + 1) * BS, head(h)],
                            shared[1, half * BS : (half + 1) * BS, head(h)],
                        ],
                        axis=0,
                    )
                    for h in heads
                ]
                for half, own in enumerate((kbuf, vbuf))
            ]
            scores = [dot_t(q_ref[rows, head(h)], k) for h, k in zip(heads, keys_of)]
            tops = [top_of([s]) for s in scores]
            weights = [weigh(s, top) for s, top in zip(scores, tops)]
            mixed = [mix(w, v) for w, v in zip(weights, values_of)]
            for n, h in enumerate(heads):
                top_ref[j, h] = tops[n]
                total_ref[j, h] = mixed[n][:, DH:]
                acc_ref[j, h] = mixed[n][:, :DH]
        return carry

    lax.fori_loop(0, blocks, step, 0)


def near(gids, picks, place, queries, keys, values, halos, from_right, pieces):
    rows = queries.shape[0]
    blocks = rows // BS
    return pl.pallas_call(
        functools.partial(near_kernel, blocks),
        out_shape=state_of(blocks),
        in_specs=[SM, SM, SM, VM] + [ANY] * 15,
        out_specs=[VM] * 3,
        scratch_shapes=[
            pltpu.VMEM(((blocks + 2) * BS, W), keys.dtype),
            pltpu.VMEM(((blocks + 2) * BS, W), keys.dtype),
            pltpu.VMEM((2, 2 * BS, W), keys.dtype),
            pltpu.VMEM((blocks, 2, BS, W), keys.dtype),
            pltpu.SemaphoreType.DMA((2, 3)),
            pltpu.SemaphoreType.DMA((4,)),
            pltpu.SemaphoreType.DMA((blocks, 2)),
        ],
        compiler_params=pltpu.CompilerParams(vmem_limit_bytes=NEAR_VMEM),
        cost_estimate=pl.CostEstimate(
            flops=rows * 6 * BS * W * 4, transcendentals=rows * 6 * BS * H, bytes_accessed=24 << 20
        ),
        name="near",
    )(gids, picks, place, queries, keys, values, *halos, *from_right, *pieces)


def score_kernel(blocks, gids, picks, q_ref, *refs):
    left, (g_o, ak_o, bk_o), refs = refs[:5], refs[5:8], refs[8:]
    top_in, total_in, acc_in, weight_ref, share_ref, acc_ref, buf, sem = refs
    g_l, ak_l, bk_l, av_l, bv_l = left
    places = first_two(gids, blocks)

    def fetch(j, carry):
        near_at = position_of(picks[j, 2], places, blocks)
        far_at = position_of(picks[j, 1], places, blocks)
        fetch_pick(near_at, (g_l.at[0], ak_l, bk_l), buf.at[j, 0], sem.at[j, 0])
        fetch_pick(far_at, (g_o.at[0], ak_o, bk_o), buf.at[j, 1], sem.at[j, 1])
        fetch_pick(near_at, (g_l.at[1], av_l, bv_l), buf.at[j, 2], sem.at[j, 2])
        return carry

    lax.fori_loop(0, blocks, fetch, 0)

    def step(j, carry):
        rows = pl.ds(pl.multiple_of(j * BS, BS), BS)
        for n in range(3):
            pltpu.make_async_copy(bk_o.at[0], buf.at[j, n], sem.at[j, n]).wait()
        q = [q_ref[rows, head(h)] for h in range(H)]
        k = [jnp.concatenate([buf[j, 0, :, head(h)], buf[j, 1, :, head(h)]], axis=0) for h in range(H)]
        v = [buf[j, 2, :, head(h)] for h in range(H)]
        old_top = [top_in[j, h] for h in range(H)]
        old_total = [total_in[j, h] for h in range(H)]
        old_acc = [acc_in[j, h] for h in range(H)]
        scores = [dot_t(q[h], k[h]) for h in range(H)]
        tops = [top_of([scores[h]], old_top[h]) for h in range(H)]
        weights = [weigh(scores[h], tops[h]) for h in range(H)]
        mixed = [dot(weights[h][:, :BS], v[h]) for h in range(H)]
        sums = [dot(weights[h], ones(2 * BS)) for h in range(H)]
        fades = [jnp.exp2((old_top[h] - tops[h]) * SCALE_LOG2) for h in range(H)]
        shares = [1.0 / (sums[h] + fades[h] * old_total[h]) for h in range(H)]
        for h in range(H):
            weight_ref[j, h] = weights[h][:, BS:]
            share_ref[j, h] = shares[h]
            acc_ref[j, h] = mixed[h] + old_acc[h] * fades[h]
        return carry

    lax.fori_loop(0, blocks, step, 0)


def score(gids, picks, queries, from_left, opposite, state):
    rows = queries.shape[0]
    blocks = rows // BS
    floats = jax.ShapeDtypeStruct((blocks, H, BS, DH), jnp.float32)
    return pl.pallas_call(
        functools.partial(score_kernel, blocks),
        out_shape=[jax.ShapeDtypeStruct((blocks, H, BS, BS), queries.dtype), floats, floats],
        in_specs=[SM, SM, VM] + [ANY] * 8 + [VM] * 3,
        out_specs=[VM] * 3,
        input_output_aliases={12: 1, 13: 2},
        scratch_shapes=[
            pltpu.VMEM((blocks, 3, BS, W), queries.dtype),
            pltpu.SemaphoreType.DMA((blocks, 3)),
        ],
        compiler_params=pltpu.CompilerParams(vmem_limit_bytes=SCORE_VMEM),
        cost_estimate=pl.CostEstimate(
            flops=rows * BS * W * 6, transcendentals=rows * 2 * BS * H, bytes_accessed=30 << 20
        ),
        name="score",
    )(gids, picks, queries, *from_left, *opposite, *state)


def last_kernel(blocks, gids, picks, g, a_v, b_v, weights, share, acc, out, buf, obuf, sem, out_sem):
    places = first_two(gids, blocks)

    def fetch(j, carry):
        fetch_pick(position_of(picks[j, 1], places, blocks), (g.at[1], a_v, b_v), buf.at[j], sem.at[j])
        return carry

    lax.fori_loop(0, blocks, fetch, 0)

    def store(j):
        rows = pl.ds(pl.multiple_of(j * BS, BS), BS)
        return pltpu.make_async_copy(obuf.at[j], out.at[rows], out_sem.at[j])

    def step(j, carry):
        pltpu.make_async_copy(b_v.at[0], buf.at[j], sem.at[j]).wait()
        mixed = [(dot(weights[j, h], buf[j, :, head(h)]) + acc[j, h]) * share[j, h] for h in range(H)]
        for h in range(H):
            obuf[j, :, head(h)] = mixed[h].astype(obuf.dtype)
        store(j).start()
        return carry

    lax.fori_loop(0, blocks, step, 0)

    def drain(j, carry):
        store(j).wait()
        return carry

    lax.fori_loop(0, blocks, drain, 0)


def last(gids, picks, parts, weights, share, acc, like):
    rows = like.shape[0]
    blocks = rows // BS
    return pl.pallas_call(
        functools.partial(last_kernel, blocks),
        out_shape=jax.ShapeDtypeStruct(like.shape, like.dtype),
        in_specs=[SM, SM] + [ANY] * 3 + [VM] * 3,
        out_specs=ANY,
        scratch_shapes=[
            pltpu.VMEM((blocks, BS, W), like.dtype),
            pltpu.VMEM((blocks, BS, W), like.dtype),
            pltpu.SemaphoreType.DMA((blocks,)),
            pltpu.SemaphoreType.DMA((blocks,)),
        ],
        compiler_params=pltpu.CompilerParams(vmem_limit_bytes=LAST_VMEM),
        cost_estimate=pl.CostEstimate(
            flops=rows * BS * W * 2, transcendentals=0, bytes_accessed=10 << 20
        ),
        name="last",
    )(gids, picks, *parts, weights, share, acc)


ALL = ("blk", "sub")


def choose_kernel(gids, place, g, g_r, g_o, g_l, keep, give_1, give_2, give_3, sem):
    blocks = QB
    rows = keep.shape[1]
    p0, p1 = lax.rem(gids[0], blocks), lax.rem(gids[1], blocks)
    slots = (0, jnp.where(p0 == p1, 0, 1))
    outs = (keep, give_1, give_2, give_3)
    for i in range(2):
        distance = lax.rem(place[i + 1] + 4, 4)
        for d, source in enumerate((g, g_r, g_o, g_l)):

            @pl.when(distance == d)
            def _(i=i, source=source):
                for n, out in enumerate(outs):
                    quarter = jnp.bitwise_xor(place[0], n)
                    half = jnp.bitwise_and(quarter, 1)
                    at = pl.ds(pl.multiple_of(jnp.right_shift(quarter, 1) * rows, rows), rows)
                    pltpu.make_async_copy(source.at[half, slots[i], at], out.at[i], sem.at[i, n]).start()

    for i in range(2):
        for n, out in enumerate(outs):
            pltpu.make_async_copy(g.at[0, 0, pl.ds(0, rows)], out.at[i], sem.at[i, n]).wait()


def choose(gids, place, g, g_r, g_o, g_l):
    piece = jax.ShapeDtypeStruct((2, BS // 2, W), g.dtype)
    return pl.pallas_call(
        choose_kernel,
        out_shape=[piece] * 4,
        in_specs=[SM, SM] + [ANY] * 4,
        out_specs=[VM] * 4,
        scratch_shapes=[pltpu.SemaphoreType.DMA((2, 4))],
        compiler_params=pltpu.CompilerParams(vmem_limit_bytes=2 << 20),
        cost_estimate=pl.CostEstimate(flops=0, transcendentals=0, bytes_accessed=1 << 20),
        name="choose",
    )(gids, place, g, g_r, g_o, g_l)


def ends_kernel(gids, g_l, ak_l, av_l, g_r, bk_r, bv_r, tail, lead, sem):
    p0, p1, _, _ = first_two(gids, QB)
    cases = (
        (0, tail, g_l, (ak_l.at[0], av_l.at[0])),
        (QB - 1, lead, g_r, (bk_r.at[B_N - 1], bv_r.at[B_N - 1])),
    )
    for n, (label, out, g, rest) in enumerate(cases):
        for half in range(2):
            done = sem.at[n, half]

            @pl.when(p0 == label)
            def _(g=g, half=half, out=out, done=done):
                pltpu.make_async_copy(g.at[half, 0], out.at[half], done).start()

            @pl.when(p1 == label)
            def _(g=g, half=half, out=out, done=done):
                pltpu.make_async_copy(g.at[half, 1], out.at[half], done).start()

            @pl.when((p0 != label) & (p1 != label))
            def _(rest=rest, half=half, out=out, done=done):
                pltpu.make_async_copy(rest[half], out.at[half], done).start()

    for n, (_, out, _, rest) in enumerate(cases):
        for half in range(2):
            pltpu.make_async_copy(rest[half], out.at[half], sem.at[n, half]).wait()


def ends(gids, g_l, ak_l, av_l, g_r, bk_r, bv_r):
    block = jax.ShapeDtypeStruct((2, BS, W), g_l.dtype)
    return pl.pallas_call(
        ends_kernel,
        out_shape=[block] * 2,
        in_specs=[SM] + [ANY] * 6,
        out_specs=[VM] * 2,
        scratch_shapes=[pltpu.SemaphoreType.DMA((2, 2))],
        compiler_params=pltpu.CompilerParams(vmem_limit_bytes=2 << 20),
        cost_estimate=pl.CostEstimate(flops=0, transcendentals=0, bytes_accessed=1 << 20),
        name="ends",
    )(gids, g_l, ak_l, av_l, g_r, bk_r, bv_r)


def swap(value, bits):
    count = lax.axis_size(ALL)
    return lax.ppermute(value, ALL, [(i, i ^ bits) for i in range(count)])


def pick_slots(mask, a, b):
    return jnp.where(mask[:, None, None], a, b)


def spread(quarters, me, owners):
    value = quarters[0]
    differ = (me ^ owners) & 3
    given = [swap(quarters[n], n) for n in (1, 2, 3)]
    for n in (1, 2, 3):
        value = pick_slots(differ == n, given[n - 1], value)
    for bit in (2, 3, 4, 5):
        same = ((me >> bit) & 1) == ((owners >> bit) & 1)
        value = pick_slots(same, value, swap(value, 1 << bit))
    return [value] + [swap(value, n) for n in (1, 2, 3)]


def whole(queries, keys, values, global_ids, rand_pick):
    rows, width = queries.shape
    blocks = rows // BS
    count = lax.axis_size("blk")
    quarter = count // 4
    right = [(i, (i + quarter) % count) for i in range(count)]
    left = [(i, (i - quarter) % count) for i in range(count)]
    everyone = lax.axis_size(ALL)

    def to_right(v):
        return lax.ppermute(v, "blk", right)

    def to_left(v):
        return lax.ppermute(v, "blk", left)

    plane = everyone // 4

    def along(v, pairs):
        return lax.ppermute(
            v, ALL, [(p * plane + i, p * plane + j) for p in range(4) for i, j in pairs]
        )

    key_blocks = keys.reshape(blocks, BS, width)
    value_blocks = values.reshape(blocks, BS, width)
    (g,) = pack(global_ids, key_blocks, value_blocks, 0, G_N, joined=True)
    g_l, g_r = to_right(g), to_left(g)
    ak, av, tail, lead = pack(global_ids, key_blocks, value_blocks, G_N, A_N, ends=True)
    bk, bv = pack(global_ids, key_blocks, value_blocks, G_N + A_N, B_N)
    ak_l, av_l = to_right(ak), to_right(av)
    bk_r, bv_r = to_left(bk), to_left(bv)
    low = along(tail, [(i, i + 1) for i in range(plane - 1)])
    high = along(lead, [(i + 1, i) for i in range(plane - 1)])
    g_o = to_right(g_l)
    bk_l, bv_l = to_right(bk), to_right(bv)
    ak_r, av_r = to_left(ak), to_left(av)
    ak_o, bk_o = to_right(ak_l), to_left(bk_r)
    av_o, bv_o = to_right(av_l), to_left(bv_r)

    me = lax.axis_index(ALL)
    owners = global_ids // blocks
    distance = owners // plane - me // plane
    spot = me % plane
    edge = jnp.where(spot == 0, 0, jnp.where(spot == plane - 1, 1, 2))
    place = jnp.stack([me & 3, distance[0], distance[1], edge])
    far_tail, far_lead = ends(global_ids, g_l, ak_l, av_l, g_r, bk_r, bv_r)
    first = along(far_tail, [(plane - 1, 0)])
    final = along(far_lead, [(0, plane - 1)])
    quarters = choose(global_ids, place, g, g_r, g_o, g_l)
    pieces = spread(quarters, me, owners)

    state = near(
        global_ids,
        rand_pick,
        place,
        queries,
        keys,
        values,
        (low, high, first, final),
        (g_r, ak_r, bk_r, av_r, bv_r),
        pieces,
    )
    weights, share, acc = score(
        global_ids,
        rand_pick,
        queries,
        (g_l, ak_l, bk_l, av_l, bv_l),
        (g_o, ak_o, bk_o),
        state,
    )
    return last(global_ids, rand_pick, (g_o, av_o, bv_o), weights, share, acc, queries)


def solution(mesh):
    return jax.shard_map(
        whole,
        mesh=mesh,
        in_specs=(
            P(("blk", "sub"), None),
            P(("blk", "sub"), None),
            P(("blk", "sub"), None),
            P(),
            P(("blk", "sub"), None),
        ),
        out_specs=P(("blk", "sub"), None),
        check_vma=False,
    )
```

```python
import functools
import math

import jax
import jax.numpy as jnp
from jax import lax
from jax.experimental import pallas as pl
from jax.experimental.pallas import tpu as pltpu
from jax.sharding import PartitionSpec as P


H = 4
DH = 128
BS = 128
QB = 16
W = H * DH
SCALE_LOG2 = math.log2(math.e) / math.sqrt(DH)
G_N, A_N, B_N = 2, 6, 8
NEAR_VMEM, SCORE_VMEM, LAST_VMEM = 24 << 20, 24 << 20, 12 << 20
ANY = pl.BlockSpec(memory_space=pl.ANY)
VM = pl.BlockSpec(memory_space=pltpu.VMEM)
SM = pl.BlockSpec(memory_space=pltpu.SMEM)
HB = pl.BlockSpec(memory_space=pltpu.HBM)


def first_two(gids, blocks):
    p0 = blocks - 1 - lax.rem(gids[0], blocks)
    p1 = blocks - 1 - lax.rem(gids[1], blocks)
    p1 = jnp.where(p1 == p0, lax.rem(p0 + 1, blocks), p1)
    return p0, p1, jnp.minimum(p0, p1), jnp.maximum(p0, p1)


def block_at(position, places, blocks):
    p0, p1, low, high = places
    if position == 0:
        return blocks - 1 - p0
    if position == 1:
        return blocks - 1 - p1
    k = position - 2
    k = k + (k >= low).astype(jnp.int32)
    return blocks - 1 - (k + (k >= high).astype(jnp.int32))


def position_of(block, places, blocks):
    p0, p1, low, high = places
    label = blocks - 1 - block
    rest = label - (label > low).astype(jnp.int32) - (label > high).astype(jnp.int32) + 2
    return jnp.where(label == p0, 0, jnp.where(label == p1, 1, rest))


def pack_kernel(start, count, joined, ends, gids, keys, values, *refs):
    blocks = keys.shape[0]
    places = first_two(gids, blocks)
    outs, (buf, in_sem, out_sem) = refs[:-3], refs[-3:]
    if joined:
        buf = outs[0]
    wanted = [block_at(start + i, places, blocks) for i in range(count)]
    if ends:
        wanted += [blocks - 1, 0]
    loads, stores = [], []
    for half, ref in enumerate((keys, values)):
        for i, block in enumerate(wanted):
            copy = pltpu.make_async_copy(ref.at[block], buf.at[half, i], in_sem.at[half, i])
            copy.start()
            loads.append((half, i, copy))
    for half, i, load in loads:
        load.wait()
        if joined:
            continue
        target = outs[half].at[i] if i < count else outs[2 + i - count].at[half]
        copy = pltpu.make_async_copy(buf.at[half, i], target, out_sem.at[half, i])
        copy.start()
        stores.append(copy)
    for copy in stores:
        copy.wait()


def pack(gids, keys, values, start, count, joined=False, ends=False):
    shapes = [jax.ShapeDtypeStruct((count, BS, W), keys.dtype)] * 2
    if joined:
        shapes = [jax.ShapeDtypeStruct((2, count, BS, W), keys.dtype)]
    if ends:
        shapes += [jax.ShapeDtypeStruct((2, BS, W), keys.dtype)] * 2
    places = count + 2 * ends
    return pl.pallas_call(
        functools.partial(pack_kernel, start, count, joined, ends),
        out_shape=shapes,
        in_specs=[SM, HB, HB],
        out_specs=[VM if joined else ANY] * len(shapes),
        scratch_shapes=[
            pltpu.VMEM((2, 1 if joined else places, BS, W), keys.dtype),
            pltpu.SemaphoreType.DMA((2, places)),
            pltpu.SemaphoreType.DMA((2, places)),
        ],
        compiler_params=pltpu.CompilerParams(vmem_limit_bytes=56 << 20),
        cost_estimate=pl.CostEstimate(
            flops=0, transcendentals=0, bytes_accessed=places * 4 * BS * W * 2
        ),
        name="pack",
    )(gids, keys, values)


def dot_t(a, b):
    return lax.dot_general(a, b, (((1,), (1,)), ((), ())), preferred_element_type=jnp.float32)


def dot(a, b):
    return lax.dot_general(a, b, (((1,), (0,)), ((), ())), preferred_element_type=jnp.float32)


def head(h):
    return slice(h * DH, (h + 1) * DH)


def wide(column):
    return jnp.broadcast_to(column, (BS, DH))


def ones(rows):
    return jnp.ones((rows, DH), jnp.bfloat16)


def top_of(scores, old=None):
    tops = [jnp.max(s, axis=1, keepdims=True) for s in scores]
    top = wide(functools.reduce(jnp.maximum, tops))
    return top if old is None else jnp.maximum(top, old)


def weigh(s, top):
    parts = [
        jnp.exp2((s[:, n : n + DH] - top) * SCALE_LOG2) for n in range(0, s.shape[1], DH)
    ]
    return jnp.concatenate(parts, axis=1).astype(jnp.bfloat16)


def mix(w, v):
    return dot(w, jnp.concatenate([v, ones(v.shape[0])], axis=1))


def state_of(blocks):
    return [jax.ShapeDtypeStruct((blocks, H, BS, DH), jnp.float32)] * 3


def fetch_pick(position, parts, dst, sem):
    at = 0
    for part in parts:
        count = part.shape[0]

        @pl.when((position >= at) & (position < at + count))
        def _(part=part, at=at, count=count):
            pltpu.make_async_copy(part.at[jnp.clip(position - at, 0, count - 1)], dst, sem).start()

        at += count


def near_kernel(blocks, gids, picks, place, q_ref, keys, values, low, high, first, last, *refs):
    sides, refs = (refs[:5], refs[5:10]), refs[10:]
    top_ref, total_ref, acc_ref, kbuf, vbuf, buf, sem, pick_sem = refs
    places = first_two(gids, blocks)
    copies = []
    for half, (ref, dst) in enumerate(((keys, kbuf), (values, vbuf))):
        copies.append(pltpu.make_async_copy(ref, dst.at[pl.ds(BS, blocks * BS)], sem.at[half, 0]))
    for copy in copies:
        copy.start()
    halos = (
        (1, place[3] == 0, first, low, 0),
        (2, place[3] == 1, last, high, (blocks + 1) * BS),
    )
    for n, wraps, there, here, at in halos:
        for half, dst in enumerate((kbuf, vbuf)):

            @pl.when(wraps)
            def _(there=there, half=half, dst=dst, at=at, n=n):
                pltpu.make_async_copy(there.at[half], dst.at[pl.ds(at, BS)], sem.at[half, n]).start()

            @pl.when(jnp.logical_not(wraps))
            def _(here=here, half=half, dst=dst, at=at, n=n):
                pltpu.make_async_copy(here.at[half], dst.at[pl.ds(at, BS)], sem.at[half, n]).start()

    def fetch(j, carry):
        for side, column in ((0, 0), (1, 2)):
            g, a_k, b_k, a_v, b_v = sides[side]
            position = position_of(picks[j, column], places, blocks)
            fetch_pick(position, (g.at[0], a_k, b_k), buf.at[j, 0, side], pick_sem.at[j, 0, side])
            fetch_pick(position, (g.at[1], a_v, b_v), buf.at[j, 1, side], pick_sem.at[j, 1, side])
        return carry

    lax.fori_loop(0, blocks, fetch, 0)
    for copy in copies:
        copy.wait()
    for n, _, _, here, at in halos:
        for half, dst in enumerate((kbuf, vbuf)):
            pltpu.make_async_copy(here.at[half], dst.at[pl.ds(at, BS)], sem.at[half, n]).wait()

    def step(j, carry):
        rows = pl.ds(pl.multiple_of(j * BS, BS), BS)
        span = pl.ds(pl.multiple_of(j * BS, BS), 3 * BS)
        for half in range(2):
            for side in range(2):
                pltpu.make_async_copy(
                    sides[side][2].at[0], buf.at[j, half, side], pick_sem.at[j, half, side]
                ).wait()
        keys_of, values_of = [
            [
                jnp.concatenate(
                    [own[span, head(h)], buf[j, half, 0, :, head(h)], buf[j, half, 1, :, head(h)]],
                    axis=0,
                )
                for h in range(H)
            ]
            for half, own in enumerate((kbuf, vbuf))
        ]
        scores = [dot_t(q_ref[rows, head(h)], keys_of[h]) for h in range(H)]
        tops = [top_of([s]) for s in scores]
        weights = [weigh(s, top) for s, top in zip(scores, tops)]
        mixed = [mix(w, v) for w, v in zip(weights, values_of)]
        for h in range(H):
            top_ref[j, h] = tops[h]
            total_ref[j, h] = mixed[h][:, DH:]
            acc_ref[j, h] = mixed[h][:, :DH]
        return carry

    lax.fori_loop(0, blocks, step, 0)


def near(gids, picks, place, queries, keys, values, halos, from_right, from_left):
    rows = queries.shape[0]
    blocks = rows // BS
    return pl.pallas_call(
        functools.partial(near_kernel, blocks),
        out_shape=state_of(blocks),
        in_specs=[SM, SM, SM, VM] + [ANY] * 16,
        out_specs=[VM] * 3,
        scratch_shapes=[
            pltpu.VMEM(((blocks + 2) * BS, W), keys.dtype),
            pltpu.VMEM(((blocks + 2) * BS, W), keys.dtype),
            pltpu.VMEM((blocks, 2, 2, BS, W), keys.dtype),
            pltpu.SemaphoreType.DMA((2, 3)),
            pltpu.SemaphoreType.DMA((blocks, 2, 2)),
        ],
        compiler_params=pltpu.CompilerParams(vmem_limit_bytes=NEAR_VMEM),
        cost_estimate=pl.CostEstimate(
            flops=rows * 5 * BS * W * 4, transcendentals=rows * 5 * BS * H, bytes_accessed=26 << 20
        ),
        name="near",
    )(gids, picks, place, queries, keys, values, *halos, *from_right, *from_left)


def score_kernel(blocks, gids, picks, place, q_ref, *refs):
    pieces, (g_o, ak_o, bk_o), refs = refs[:4], refs[4:7], refs[7:]
    top_in, total_in, acc_in, weight_ref, share_ref, acc_ref, shared, buf, shared_sem, sem = refs
    places = first_two(gids, blocks)
    copies = []
    for n, piece in enumerate(pieces):
        quarter = jnp.bitwise_and(jnp.bitwise_xor(place[0], n), 3)
        rows = piece.shape[1]
        start = jnp.bitwise_and(quarter, 1) * (2 * rows) + jnp.right_shift(quarter, 1) * rows
        at = pl.ds(pl.multiple_of(start, rows), rows)
        copies.append(pltpu.make_async_copy(piece, shared.at[:, at], shared_sem.at[n]))
    for copy in copies:
        copy.start()

    def fetch(j, carry):
        position = position_of(picks[j, 1], places, blocks)
        fetch_pick(position, (g_o.at[0], ak_o, bk_o), buf.at[j], sem.at[j])
        return carry

    lax.fori_loop(0, blocks, fetch, 0)
    for copy in copies:
        copy.wait()

    def step(j, carry):
        rows = pl.ds(pl.multiple_of(j * BS, BS), BS)
        pltpu.make_async_copy(bk_o.at[0], buf.at[j], sem.at[j]).wait()
        q = [q_ref[rows, head(h)] for h in range(H)]
        k = [
            jnp.concatenate(
                [shared[0, :BS, head(h)], shared[1, :BS, head(h)], buf[j, :, head(h)]], axis=0
            )
            for h in range(H)
        ]
        v = [jnp.concatenate([shared[n, BS:, head(h)] for n in range(2)], axis=0) for h in range(H)]
        old_top = [top_in[j, h] for h in range(H)]
        old_total = [total_in[j, h] for h in range(H)]
        old_acc = [acc_in[j, h] for h in range(H)]
        scores = [dot_t(q[h], k[h]) for h in range(H)]
        tops = [top_of([scores[h]], old_top[h]) for h in range(H)]
        weights = [weigh(scores[h], tops[h]) for h in range(H)]
        mixed = [mix(weights[h][:, : 2 * BS], v[h]) for h in range(H)]
        sums = [mixed[h][:, DH:] + dot(weights[h][:, 2 * BS :], ones(BS)) for h in range(H)]
        fades = [jnp.exp2((old_top[h] - tops[h]) * SCALE_LOG2) for h in range(H)]
        shares = [1.0 / (sums[h] + fades[h] * old_total[h]) for h in range(H)]
        for h in range(H):
            weight_ref[j, h] = weights[h][:, 2 * BS :]
            share_ref[j, h] = shares[h]
            acc_ref[j, h] = mixed[h][:, :DH] + old_acc[h] * fades[h]
        return carry

    lax.fori_loop(0, blocks, step, 0)


def score(gids, picks, place, queries, pieces, opposite, state):
    rows = queries.shape[0]
    blocks = rows // BS
    floats = jax.ShapeDtypeStruct((blocks, H, BS, DH), jnp.float32)
    return pl.pallas_call(
        functools.partial(score_kernel, blocks),
        out_shape=[jax.ShapeDtypeStruct((blocks, H, BS, BS), queries.dtype), floats, floats],
        in_specs=[SM, SM, SM, VM] + [ANY] * 7 + [VM] * 3,
        out_specs=[VM] * 3,
        input_output_aliases={12: 1, 13: 2},
        scratch_shapes=[
            pltpu.VMEM((2, 2 * BS, W), queries.dtype),
            pltpu.VMEM((blocks, BS, W), queries.dtype),
            pltpu.SemaphoreType.DMA((4,)),
            pltpu.SemaphoreType.DMA((blocks,)),
        ],
        compiler_params=pltpu.CompilerParams(vmem_limit_bytes=SCORE_VMEM),
        cost_estimate=pl.CostEstimate(
            flops=rows * BS * W * 10, transcendentals=rows * 3 * BS * H, bytes_accessed=28 << 20
        ),
        name="score",
    )(gids, picks, place, queries, *pieces, *opposite, *state)


def last_kernel(blocks, gids, picks, g, a_v, b_v, weights, share, acc, out, buf, obuf, sem, out_sem):
    places = first_two(gids, blocks)

    def fetch(j, carry):
        fetch_pick(position_of(picks[j, 1], places, blocks), (g.at[1], a_v, b_v), buf.at[j], sem.at[j])
        return carry

    lax.fori_loop(0, blocks, fetch, 0)

    def store(j):
        rows = pl.ds(pl.multiple_of(j * BS, BS), BS)
        return pltpu.make_async_copy(obuf.at[j], out.at[rows], out_sem.at[j])

    def step(j, carry):
        pltpu.make_async_copy(b_v.at[0], buf.at[j], sem.at[j]).wait()
        mixed = [(dot(weights[j, h], buf[j, :, head(h)]) + acc[j, h]) * share[j, h] for h in range(H)]
        for h in range(H):
            obuf[j, :, head(h)] = mixed[h].astype(obuf.dtype)
        store(j).start()
        return carry

    lax.fori_loop(0, blocks, step, 0)

    def drain(j, carry):
        store(j).wait()
        return carry

    lax.fori_loop(0, blocks, drain, 0)


def last(gids, picks, parts, weights, share, acc, like):
    rows = like.shape[0]
    blocks = rows // BS
    return pl.pallas_call(
        functools.partial(last_kernel, blocks),
        out_shape=jax.ShapeDtypeStruct(like.shape, like.dtype),
        in_specs=[SM, SM] + [ANY] * 3 + [VM] * 3,
        out_specs=ANY,
        scratch_shapes=[
            pltpu.VMEM((blocks, BS, W), like.dtype),
            pltpu.VMEM((blocks, BS, W), like.dtype),
            pltpu.SemaphoreType.DMA((blocks,)),
            pltpu.SemaphoreType.DMA((blocks,)),
        ],
        compiler_params=pltpu.CompilerParams(vmem_limit_bytes=LAST_VMEM),
        cost_estimate=pl.CostEstimate(
            flops=rows * BS * W * 2, transcendentals=0, bytes_accessed=10 << 20
        ),
        name="last",
    )(gids, picks, *parts, weights, share, acc)


ALL = ("blk", "sub")


def choose_kernel(gids, place, g, g_r, g_o, g_l, keep, give_1, give_2, give_3, sem):
    blocks = QB
    rows = keep.shape[1]
    p0, p1 = lax.rem(gids[0], blocks), lax.rem(gids[1], blocks)
    slots = (0, jnp.where(p0 == p1, 0, 1))
    outs = (keep, give_1, give_2, give_3)
    for i in range(2):
        distance = lax.rem(place[i + 1] + 4, 4)
        for d, source in enumerate((g, g_r, g_o, g_l)):

            @pl.when(distance == d)
            def _(i=i, source=source):
                for n, out in enumerate(outs):
                    quarter = jnp.bitwise_xor(place[0], n)
                    half = jnp.bitwise_and(quarter, 1)
                    at = pl.ds(pl.multiple_of(jnp.right_shift(quarter, 1) * rows, rows), rows)
                    pltpu.make_async_copy(source.at[half, slots[i], at], out.at[i], sem.at[i, n]).start()

    for i in range(2):
        for n, out in enumerate(outs):
            pltpu.make_async_copy(g.at[0, 0, pl.ds(0, rows)], out.at[i], sem.at[i, n]).wait()


def choose(gids, place, g, g_r, g_o, g_l):
    piece = jax.ShapeDtypeStruct((2, BS // 2, W), g.dtype)
    return pl.pallas_call(
        choose_kernel,
        out_shape=[piece] * 4,
        in_specs=[SM, SM] + [ANY] * 4,
        out_specs=[VM] * 4,
        scratch_shapes=[pltpu.SemaphoreType.DMA((2, 4))],
        compiler_params=pltpu.CompilerParams(vmem_limit_bytes=2 << 20),
        cost_estimate=pl.CostEstimate(flops=0, transcendentals=0, bytes_accessed=1 << 20),
        name="choose",
    )(gids, place, g, g_r, g_o, g_l)


def ends_kernel(gids, g_l, ak_l, av_l, g_r, bk_r, bv_r, tail, lead, sem):
    p0, p1, _, _ = first_two(gids, QB)
    cases = (
        (0, tail, g_l, (ak_l.at[0], av_l.at[0])),
        (QB - 1, lead, g_r, (bk_r.at[B_N - 1], bv_r.at[B_N - 1])),
    )
    for n, (label, out, g, rest) in enumerate(cases):
        for half in range(2):
            done = sem.at[n, half]

            @pl.when(p0 == label)
            def _(g=g, half=half, out=out, done=done):
                pltpu.make_async_copy(g.at[half, 0], out.at[half], done).start()

            @pl.when(p1 == label)
            def _(g=g, half=half, out=out, done=done):
                pltpu.make_async_copy(g.at[half, 1], out.at[half], done).start()

            @pl.when((p0 != label) & (p1 != label))
            def _(rest=rest, half=half, out=out, done=done):
                pltpu.make_async_copy(rest[half], out.at[half], done).start()

    for n, (_, out, _, rest) in enumerate(cases):
        for half in range(2):
            pltpu.make_async_copy(rest[half], out.at[half], sem.at[n, half]).wait()


def ends(gids, g_l, ak_l, av_l, g_r, bk_r, bv_r):
    block = jax.ShapeDtypeStruct((2, BS, W), g_l.dtype)
    return pl.pallas_call(
        ends_kernel,
        out_shape=[block] * 2,
        in_specs=[SM] + [ANY] * 6,
        out_specs=[VM] * 2,
        scratch_shapes=[pltpu.SemaphoreType.DMA((2, 2))],
        compiler_params=pltpu.CompilerParams(vmem_limit_bytes=2 << 20),
        cost_estimate=pl.CostEstimate(flops=0, transcendentals=0, bytes_accessed=1 << 20),
        name="ends",
    )(gids, g_l, ak_l, av_l, g_r, bk_r, bv_r)


def swap(value, bits):
    count = lax.axis_size(ALL)
    return lax.ppermute(value, ALL, [(i, i ^ bits) for i in range(count)])


def pick_slots(mask, a, b):
    return jnp.where(mask[:, None, None], a, b)


def spread(quarters, me, owners):
    value = quarters[0]
    differ = (me ^ owners) & 3
    given = [swap(quarters[n], n) for n in (1, 2, 3)]
    for n in (1, 2, 3):
        value = pick_slots(differ == n, given[n - 1], value)
    for bit in (2, 3, 4, 5):
        same = ((me >> bit) & 1) == ((owners >> bit) & 1)
        value = pick_slots(same, value, swap(value, 1 << bit))
    return [value] + [swap(value, n) for n in (1, 2, 3)]


def whole(queries, keys, values, global_ids, rand_pick):
    rows, width = queries.shape
    blocks = rows // BS
    count = lax.axis_size("blk")
    quarter = count // 4
    right = [(i, (i + quarter) % count) for i in range(count)]
    left = [(i, (i - quarter) % count) for i in range(count)]
    everyone = lax.axis_size(ALL)

    def to_right(v):
        return lax.ppermute(v, "blk", right)

    def to_left(v):
        return lax.ppermute(v, "blk", left)

    plane = everyone // 4

    def along(v, pairs):
        return lax.ppermute(
            v, ALL, [(p * plane + i, p * plane + j) for p in range(4) for i, j in pairs]
        )

    key_blocks = keys.reshape(blocks, BS, width)
    value_blocks = values.reshape(blocks, BS, width)
    (g,) = pack(global_ids, key_blocks, value_blocks, 0, G_N, joined=True)
    g_l, g_r = to_right(g), to_left(g)
    ak, av, tail, lead = pack(global_ids, key_blocks, value_blocks, G_N, A_N, ends=True)
    bk, bv = pack(global_ids, key_blocks, value_blocks, G_N + A_N, B_N)
    ak_l, av_l = to_right(ak), to_right(av)
    bk_r, bv_r = to_left(bk), to_left(bv)
    low = along(tail, [(i, i + 1) for i in range(plane - 1)])
    high = along(lead, [(i + 1, i) for i in range(plane - 1)])
    g_o = to_right(g_l)
    bk_l, bv_l = to_right(bk), to_right(bv)
    ak_r, av_r = to_left(ak), to_left(av)
    ak_o, bk_o = to_right(ak_l), to_left(bk_r)
    av_o, bv_o = to_right(av_l), to_left(bv_r)

    me = lax.axis_index(ALL)
    owners = global_ids // blocks
    distance = owners // plane - me // plane
    spot = me % plane
    edge = jnp.where(spot == 0, 0, jnp.where(spot == plane - 1, 1, 2))
    place = jnp.stack([me & 3, distance[0], distance[1], edge])
    far_tail, far_lead = ends(global_ids, g_l, ak_l, av_l, g_r, bk_r, bv_r)
    first = along(far_tail, [(plane - 1, 0)])
    final = along(far_lead, [(0, plane - 1)])
    quarters = choose(global_ids, place, g, g_r, g_o, g_l)
    pieces = spread(quarters, me, owners)

    state = near(
        global_ids,
        rand_pick,
        place,
        queries,
        keys,
        values,
        (low, high, first, final),
        (g_r, ak_r, bk_r, av_r, bv_r),
        (g_l, ak_l, bk_l, av_l, bv_l),
    )
    weights, share, acc = score(
        global_ids, rand_pick, place, queries, pieces, (g_o, ak_o, bk_o), state
    )
    return last(global_ids, rand_pick, (g_o, av_o, bv_o), weights, share, acc, queries)


def solution(mesh):
    return jax.shard_map(
        whole,
        mesh=mesh,
        in_specs=(
            P(("blk", "sub"), None),
            P(("blk", "sub"), None),
            P(("blk", "sub"), None),
            P(),
            P(("blk", "sub"), None),
        ),
        out_specs=P(("blk", "sub"), None),
        check_vma=False,
    )
```

```python
import functools
import math

import jax
import jax.numpy as jnp
from jax import lax
from jax.experimental import pallas as pl
from jax.experimental.pallas import tpu as pltpu
from jax.sharding import PartitionSpec as P


H = 4
DH = 128
BS = 128
QB = 16
W = H * DH
SCALE_LOG2 = math.log2(math.e) / math.sqrt(DH)
G_N, A_N, B_N = 2, 6, 8
NEAR_VMEM, SCORE_VMEM, LAST_VMEM = 41 << 20, 24 << 20, 12 << 20
ANY = pl.BlockSpec(memory_space=pl.ANY)
VM = pl.BlockSpec(memory_space=pltpu.VMEM)
SM = pl.BlockSpec(memory_space=pltpu.SMEM)
HB = pl.BlockSpec(memory_space=pltpu.HBM)


def first_two(gids, blocks):
    p0 = blocks - 1 - lax.rem(gids[0], blocks)
    p1 = blocks - 1 - lax.rem(gids[1], blocks)
    p1 = jnp.where(p1 == p0, lax.rem(p0 + 1, blocks), p1)
    return p0, p1, jnp.minimum(p0, p1), jnp.maximum(p0, p1)


def block_at(position, places, blocks):
    p0, p1, low, high = places
    if position == 0:
        return blocks - 1 - p0
    if position == 1:
        return blocks - 1 - p1
    k = position - 2
    k = k + (k >= low).astype(jnp.int32)
    return blocks - 1 - (k + (k >= high).astype(jnp.int32))


def position_of(block, places, blocks):
    p0, p1, low, high = places
    label = blocks - 1 - block
    rest = label - (label > low).astype(jnp.int32) - (label > high).astype(jnp.int32) + 2
    return jnp.where(label == p0, 0, jnp.where(label == p1, 1, rest))


def pack_kernel(start, count, joined, ends, gids, keys, values, *refs):
    blocks = keys.shape[0]
    places = first_two(gids, blocks)
    outs, (buf, in_sem, out_sem) = refs[:-3], refs[-3:]
    if joined:
        buf = outs[0]
    wanted = [block_at(start + i, places, blocks) for i in range(count)]
    if ends:
        wanted += [blocks - 1, 0]
    loads, stores = [], []
    for half, ref in enumerate((keys, values)):
        for i, block in enumerate(wanted):
            copy = pltpu.make_async_copy(ref.at[block], buf.at[half, i], in_sem.at[half, i])
            copy.start()
            loads.append((half, i, copy))
    for half, i, load in loads:
        load.wait()
        if joined:
            continue
        target = outs[half].at[i] if i < count else outs[2 + i - count].at[half]
        copy = pltpu.make_async_copy(buf.at[half, i], target, out_sem.at[half, i])
        copy.start()
        stores.append(copy)
    for copy in stores:
        copy.wait()


def pack(gids, keys, values, start, count, joined=False, ends=False):
    shapes = [jax.ShapeDtypeStruct((count, BS, W), keys.dtype)] * 2
    if joined:
        shapes = [jax.ShapeDtypeStruct((2, count, BS, W), keys.dtype)]
    if ends:
        shapes += [jax.ShapeDtypeStruct((2, BS, W), keys.dtype)] * 2
    places = count + 2 * ends
    return pl.pallas_call(
        functools.partial(pack_kernel, start, count, joined, ends),
        out_shape=shapes,
        in_specs=[SM, HB, HB],
        out_specs=[VM if joined else ANY] * len(shapes),
        scratch_shapes=[
            pltpu.VMEM((2, 1 if joined else places, BS, W), keys.dtype),
            pltpu.SemaphoreType.DMA((2, places)),
            pltpu.SemaphoreType.DMA((2, places)),
        ],
        compiler_params=pltpu.CompilerParams(vmem_limit_bytes=56 << 20),
        cost_estimate=pl.CostEstimate(
            flops=0, transcendentals=0, bytes_accessed=places * 4 * BS * W * 2
        ),
        name="pack",
    )(gids, keys, values)


def dot_t(a, b):
    return lax.dot_general(a, b, (((1,), (1,)), ((), ())), preferred_element_type=jnp.float32)


def dot(a, b):
    return lax.dot_general(a, b, (((1,), (0,)), ((), ())), preferred_element_type=jnp.float32)


def head(h):
    return slice(h * DH, (h + 1) * DH)


def wide(column):
    return jnp.broadcast_to(column, (BS, DH))


def ones(rows):
    return jnp.ones((rows, DH), jnp.bfloat16)


def top_of(scores, old=None):
    tops = [jnp.max(s, axis=1, keepdims=True) for s in scores]
    top = wide(functools.reduce(jnp.maximum, tops))
    return top if old is None else jnp.maximum(top, old)


def weigh(s, top):
    parts = [
        jnp.exp2((s[:, n : n + DH] - top) * SCALE_LOG2) for n in range(0, s.shape[1], DH)
    ]
    return jnp.concatenate(parts, axis=1).astype(jnp.bfloat16)


def mix(w, v):
    return dot(w, jnp.concatenate([v, ones(v.shape[0])], axis=1))


def state_of(blocks):
    return [pltpu.VMEM((blocks, H, BS, DH), jnp.float32)] * 3


def fetch_pick(position, parts, dst, sem):
    at = 0
    for part in parts:
        count = part.shape[0]

        @pl.when((position >= at) & (position < at + count))
        def _(part=part, at=at, count=count):
            pltpu.make_async_copy(part.at[jnp.clip(position - at, 0, count - 1)], dst, sem).start()

        at += count


def near_kernel(blocks, gids, picks, place, q_ref, keys, values, low, high, first, last, *refs):
    sides, refs = (refs[:5], refs[5:10]), refs[10:]
    top_ref, total_ref, acc_ref, qbuf, kbuf, vbuf, buf, sem, pick_sem = refs
    places = first_two(gids, blocks)
    copies = [pltpu.make_async_copy(q_ref, qbuf, sem.at[0, 3])]
    for half, (ref, dst) in enumerate(((keys, kbuf), (values, vbuf))):
        copies.append(pltpu.make_async_copy(ref, dst.at[pl.ds(BS, blocks * BS)], sem.at[half, 0]))
    for copy in copies:
        copy.start()
    halos = (
        (1, place[3] == 0, first, low, 0),
        (2, place[3] == 1, last, high, (blocks + 1) * BS),
    )
    for n, wraps, there, here, at in halos:
        for half, dst in enumerate((kbuf, vbuf)):

            @pl.when(wraps)
            def _(there=there, half=half, dst=dst, at=at, n=n):
                pltpu.make_async_copy(there.at[half], dst.at[pl.ds(at, BS)], sem.at[half, n]).start()

            @pl.when(jnp.logical_not(wraps))
            def _(here=here, half=half, dst=dst, at=at, n=n):
                pltpu.make_async_copy(here.at[half], dst.at[pl.ds(at, BS)], sem.at[half, n]).start()

    def fetch(j, carry):
        for side, column in ((0, 0), (1, 2)):
            g, a_k, b_k, a_v, b_v = sides[side]
            position = position_of(picks[j, column], places, blocks)
            fetch_pick(position, (g.at[0], a_k, b_k), buf.at[j, 0, side], pick_sem.at[j, 0, side])
            fetch_pick(position, (g.at[1], a_v, b_v), buf.at[j, 1, side], pick_sem.at[j, 1, side])
        return carry

    lax.fori_loop(0, blocks, fetch, 0)
    for copy in copies:
        copy.wait()
    for n, _, _, here, at in halos:
        for half, dst in enumerate((kbuf, vbuf)):
            pltpu.make_async_copy(here.at[half], dst.at[pl.ds(at, BS)], sem.at[half, n]).wait()

    def step(j, carry):
        rows = pl.ds(pl.multiple_of(j * BS, BS), BS)
        span = pl.ds(pl.multiple_of(j * BS, BS), 3 * BS)
        for half in range(2):
            for side in range(2):
                pltpu.make_async_copy(
                    sides[side][2].at[0], buf.at[j, half, side], pick_sem.at[j, half, side]
                ).wait()
        q = [qbuf[rows, head(h)] for h in range(H)]
        own_keys = [kbuf[span, head(h)] for h in range(H)]
        own_values = [vbuf[span, head(h)] for h in range(H)]
        side_keys, side_values = [
            [
                jnp.concatenate([buf[j, half, side, :, head(h)] for side in range(2)], axis=0)
                for h in range(H)
            ]
            for half in range(2)
        ]
        own_scores = [dot_t(q[h], own_keys[h]) for h in range(H)]
        side_scores = [dot_t(q[h], side_keys[h]) for h in range(H)]
        tops = [top_of([own_scores[h], side_scores[h]]) for h in range(H)]
        own_weights = [weigh(own_scores[h], tops[h]) for h in range(H)]
        side_weights = [weigh(side_scores[h], tops[h]) for h in range(H)]
        mixed = [
            mix(own_weights[h], own_values[h]) + mix(side_weights[h], side_values[h])
            for h in range(H)
        ]
        for h in range(H):
            top_ref[j, h] = tops[h]
            total_ref[j, h] = mixed[h][:, DH:]
            acc_ref[j, h] = mixed[h][:, :DH]
        return carry

    lax.fori_loop(0, blocks, step, 0)


def near(gids, picks, place, queries, keys, values, halos, from_right, from_left):
    rows = queries.shape[0]
    blocks = rows // BS
    return pl.pallas_call(
        functools.partial(near_kernel, blocks),
        out_shape=state_of(blocks),
        in_specs=[SM, SM, SM] + [ANY] * 17,
        out_specs=[VM] * 3,
        scratch_shapes=[
            pltpu.VMEM((rows, W), keys.dtype),
            pltpu.VMEM(((blocks + 2) * BS, W), keys.dtype),
            pltpu.VMEM(((blocks + 2) * BS, W), keys.dtype),
            pltpu.VMEM((blocks, 2, 2, BS, W), keys.dtype),
            pltpu.SemaphoreType.DMA((2, 4)),
            pltpu.SemaphoreType.DMA((blocks, 2, 2)),
        ],
        compiler_params=pltpu.CompilerParams(vmem_limit_bytes=NEAR_VMEM),
        cost_estimate=pl.CostEstimate(
            flops=rows * 5 * BS * W * 4, transcendentals=rows * 5 * BS * H, bytes_accessed=26 << 20
        ),
        name="near",
    )(gids, picks, place, queries, keys, values, *halos, *from_right, *from_left)


def score_kernel(blocks, gids, picks, place, q_ref, *refs):
    pieces, (g_o, ak_o, bk_o), refs = refs[:4], refs[4:7], refs[7:]
    top_in, total_in, acc_in, weight_ref, share_ref, acc_ref, shared, buf, shared_sem, sem = refs
    places = first_two(gids, blocks)
    copies = []
    for n, piece in enumerate(pieces):
        quarter = jnp.bitwise_and(jnp.bitwise_xor(place[0], n), 3)
        rows = piece.shape[1]
        start = jnp.bitwise_and(quarter, 1) * (2 * rows) + jnp.right_shift(quarter, 1) * rows
        at = pl.ds(pl.multiple_of(start, rows), rows)
        copies.append(pltpu.make_async_copy(piece, shared.at[:, at], shared_sem.at[n]))
    for copy in copies:
        copy.start()

    def fetch(j, carry):
        position = position_of(picks[j, 1], places, blocks)
        fetch_pick(position, (g_o.at[0], ak_o, bk_o), buf.at[j], sem.at[j])
        return carry

    lax.fori_loop(0, blocks, fetch, 0)
    for copy in copies:
        copy.wait()

    def step(j, carry):
        rows = pl.ds(pl.multiple_of(j * BS, BS), BS)
        pltpu.make_async_copy(bk_o.at[0], buf.at[j], sem.at[j]).wait()
        q = [q_ref[rows, head(h)] for h in range(H)]
        k = [
            jnp.concatenate(
                [shared[0, :BS, head(h)], shared[1, :BS, head(h)], buf[j, :, head(h)]], axis=0
            )
            for h in range(H)
        ]
        v = [jnp.concatenate([shared[n, BS:, head(h)] for n in range(2)], axis=0) for h in range(H)]
        old_top = [top_in[j, h] for h in range(H)]
        old_total = [total_in[j, h] for h in range(H)]
        old_acc = [acc_in[j, h] for h in range(H)]
        scores = [dot_t(q[h], k[h]) for h in range(H)]
        tops = [top_of([scores[h]], old_top[h]) for h in range(H)]
        weights = [weigh(scores[h], tops[h]) for h in range(H)]
        mixed = [mix(weights[h][:, : 2 * BS], v[h]) for h in range(H)]
        sums = [mixed[h][:, DH:] + dot(weights[h][:, 2 * BS :], ones(BS)) for h in range(H)]
        fades = [jnp.exp2((old_top[h] - tops[h]) * SCALE_LOG2) for h in range(H)]
        shares = [1.0 / (sums[h] + fades[h] * old_total[h]) for h in range(H)]
        for h in range(H):
            weight_ref[j, h] = weights[h][:, 2 * BS :]
            share_ref[j, h] = shares[h]
            acc_ref[j, h] = mixed[h][:, :DH] + old_acc[h] * fades[h]
        return carry

    lax.fori_loop(0, blocks, step, 0)


def score(gids, picks, place, queries, pieces, opposite, state):
    rows = queries.shape[0]
    blocks = rows // BS
    floats = jax.ShapeDtypeStruct((blocks, H, BS, DH), jnp.float32)
    return pl.pallas_call(
        functools.partial(score_kernel, blocks),
        out_shape=[jax.ShapeDtypeStruct((blocks, H, BS, BS), queries.dtype), floats, floats],
        in_specs=[SM, SM, SM, VM] + [ANY] * 7 + [VM] * 3,
        out_specs=[VM] * 3,
        input_output_aliases={12: 1, 13: 2},
        scratch_shapes=[
            pltpu.VMEM((2, 2 * BS, W), queries.dtype),
            pltpu.VMEM((blocks, BS, W), queries.dtype),
            pltpu.SemaphoreType.DMA((4,)),
            pltpu.SemaphoreType.DMA((blocks,)),
        ],
        compiler_params=pltpu.CompilerParams(vmem_limit_bytes=SCORE_VMEM),
        cost_estimate=pl.CostEstimate(
            flops=rows * BS * W * 10, transcendentals=rows * 3 * BS * H, bytes_accessed=28 << 20
        ),
        name="score",
    )(gids, picks, place, queries, *pieces, *opposite, *state)


def last_kernel(blocks, gids, picks, g, a_v, b_v, weights, share, acc, out, obuf, out_sem):
    places = first_two(gids, blocks)

    def store(j):
        rows = pl.ds(pl.multiple_of(j * BS, BS), BS)
        return pltpu.make_async_copy(obuf.at[j], out.at[rows], out_sem.at[j])

    def step(j, carry):
        position = position_of(picks[j, 1], places, blocks)

        def finish(v):
            mixed = [(dot(weights[j, h], v[:, head(h)]) + acc[j, h]) * share[j, h] for h in range(H)]
            for h in range(H):
                obuf[j, :, head(h)] = mixed[h].astype(obuf.dtype)

        @pl.when(position < G_N)
        def _():
            finish(g.at[1, jnp.minimum(position, G_N - 1)])

        @pl.when((position >= G_N) & (position < G_N + A_N))
        def _():
            finish(a_v.at[jnp.clip(position - G_N, 0, A_N - 1)])

        @pl.when(position >= G_N + A_N)
        def _():
            finish(b_v.at[jnp.clip(position - G_N - A_N, 0, B_N - 1)])

        store(j).start()
        return carry

    lax.fori_loop(0, blocks, step, 0)

    def drain(j, carry):
        store(j).wait()
        return carry

    lax.fori_loop(0, blocks, drain, 0)


def last(gids, picks, parts, weights, share, acc, like):
    rows = like.shape[0]
    blocks = rows // BS
    return pl.pallas_call(
        functools.partial(last_kernel, blocks),
        out_shape=jax.ShapeDtypeStruct(like.shape, like.dtype),
        in_specs=[SM, SM] + [VM] * 6,
        out_specs=ANY,
        scratch_shapes=[
            pltpu.VMEM((blocks, BS, W), like.dtype),
            pltpu.SemaphoreType.DMA((blocks,)),
        ],
        compiler_params=pltpu.CompilerParams(vmem_limit_bytes=LAST_VMEM),
        cost_estimate=pl.CostEstimate(
            flops=rows * BS * W * 2, transcendentals=0, bytes_accessed=10 << 20
        ),
        name="last",
    )(gids, picks, *parts, weights, share, acc)


ALL = ("blk", "sub")


def choose_kernel(gids, place, g, g_r, g_o, g_l, keep, give_1, give_2, give_3, sem):
    blocks = QB
    rows = keep.shape[1]
    p0, p1 = lax.rem(gids[0], blocks), lax.rem(gids[1], blocks)
    slots = (0, jnp.where(p0 == p1, 0, 1))
    outs = (keep, give_1, give_2, give_3)
    for i in range(2):
        distance = lax.rem(place[i + 1] + 4, 4)
        for d, source in enumerate((g, g_r, g_o, g_l)):

            @pl.when(distance == d)
            def _(i=i, source=source):
                for n, out in enumerate(outs):
                    quarter = jnp.bitwise_xor(place[0], n)
                    half = jnp.bitwise_and(quarter, 1)
                    at = pl.ds(pl.multiple_of(jnp.right_shift(quarter, 1) * rows, rows), rows)
                    pltpu.make_async_copy(source.at[half, slots[i], at], out.at[i], sem.at[i, n]).start()

    for i in range(2):
        for n, out in enumerate(outs):
            pltpu.make_async_copy(g.at[0, 0, pl.ds(0, rows)], out.at[i], sem.at[i, n]).wait()


def choose(gids, place, g, g_r, g_o, g_l):
    piece = jax.ShapeDtypeStruct((2, BS // 2, W), g.dtype)
    return pl.pallas_call(
        choose_kernel,
        out_shape=[piece] * 4,
        in_specs=[SM, SM] + [ANY] * 4,
        out_specs=[VM] * 4,
        scratch_shapes=[pltpu.SemaphoreType.DMA((2, 4))],
        compiler_params=pltpu.CompilerParams(vmem_limit_bytes=56 << 20),
        cost_estimate=pl.CostEstimate(flops=0, transcendentals=0, bytes_accessed=1 << 20),
        name="choose",
    )(gids, place, g, g_r, g_o, g_l)


def ends_kernel(gids, g_l, ak_l, av_l, g_r, bk_r, bv_r, tail, lead, sem):
    p0, p1, _, _ = first_two(gids, QB)
    cases = (
        (0, tail, g_l, (ak_l.at[0], av_l.at[0])),
        (QB - 1, lead, g_r, (bk_r.at[B_N - 1], bv_r.at[B_N - 1])),
    )
    for n, (label, out, g, rest) in enumerate(cases):
        for half in range(2):
            done = sem.at[n, half]

            @pl.when(p0 == label)
            def _(g=g, half=half, out=out, done=done):
                pltpu.make_async_copy(g.at[half, 0], out.at[half], done).start()

            @pl.when(p1 == label)
            def _(g=g, half=half, out=out, done=done):
                pltpu.make_async_copy(g.at[half, 1], out.at[half], done).start()

            @pl.when((p0 != label) & (p1 != label))
            def _(rest=rest, half=half, out=out, done=done):
                pltpu.make_async_copy(rest[half], out.at[half], done).start()

    for n, (_, out, _, rest) in enumerate(cases):
        for half in range(2):
            pltpu.make_async_copy(rest[half], out.at[half], sem.at[n, half]).wait()


def ends(gids, g_l, ak_l, av_l, g_r, bk_r, bv_r):
    block = jax.ShapeDtypeStruct((2, BS, W), g_l.dtype)
    return pl.pallas_call(
        ends_kernel,
        out_shape=[block] * 2,
        in_specs=[SM] + [ANY] * 6,
        out_specs=[VM] * 2,
        scratch_shapes=[pltpu.SemaphoreType.DMA((2, 2))],
        compiler_params=pltpu.CompilerParams(vmem_limit_bytes=8 << 20),
        cost_estimate=pl.CostEstimate(flops=0, transcendentals=0, bytes_accessed=1 << 20),
        name="ends",
    )(gids, g_l, ak_l, av_l, g_r, bk_r, bv_r)


def swap(value, bits):
    count = lax.axis_size(ALL)
    return lax.ppermute(value, ALL, [(i, i ^ bits) for i in range(count)])


def pick_slots(mask, a, b):
    return jnp.where(mask[:, None, None], a, b)


def spread(quarters, me, owners):
    value = quarters[0]
    differ = (me ^ owners) & 3
    given = [swap(quarters[n], n) for n in (1, 2, 3)]
    for n in (1, 2, 3):
        value = pick_slots(differ == n, given[n - 1], value)
    for bit in (2, 3, 4, 5):
        same = ((me >> bit) & 1) == ((owners >> bit) & 1)
        value = pick_slots(same, value, swap(value, 1 << bit))
    return [value] + [swap(value, n) for n in (1, 2, 3)]


def whole(queries, keys, values, global_ids, rand_pick):
    rows, width = queries.shape
    blocks = rows // BS
    count = lax.axis_size("blk")
    quarter = count // 4
    right = [(i, (i + quarter) % count) for i in range(count)]
    left = [(i, (i - quarter) % count) for i in range(count)]
    everyone = lax.axis_size(ALL)

    def to_right(v):
        return lax.ppermute(v, "blk", right)

    def to_left(v):
        return lax.ppermute(v, "blk", left)

    plane = everyone // 4

    def along(v, pairs):
        return lax.ppermute(
            v, ALL, [(p * plane + i, p * plane + j) for p in range(4) for i, j in pairs]
        )

    key_blocks = keys.reshape(blocks, BS, width)
    value_blocks = values.reshape(blocks, BS, width)
    (g,) = pack(global_ids, key_blocks, value_blocks, 0, G_N, joined=True)
    g_l, g_r = to_right(g), to_left(g)
    ak, av, tail, lead = pack(global_ids, key_blocks, value_blocks, G_N, A_N, ends=True)
    bk, bv = pack(global_ids, key_blocks, value_blocks, G_N + A_N, B_N)
    ak_l, av_l = to_right(ak), to_right(av)
    bk_r, bv_r = to_left(bk), to_left(bv)
    low = along(tail, [(i, i + 1) for i in range(plane - 1)])
    high = along(lead, [(i + 1, i) for i in range(plane - 1)])
    g_o = to_right(g_l)
    bk_l, bv_l = to_right(bk), to_right(bv)
    ak_r, av_r = to_left(ak), to_left(av)
    ak_o, bk_o = to_right(ak_l), to_left(bk_r)
    av_o, bv_o = to_right(av_l), to_left(bv_r)

    me = lax.axis_index(ALL)
    owners = global_ids // blocks
    distance = owners // plane - me // plane
    spot = me % plane
    edge = jnp.where(spot == 0, 0, jnp.where(spot == plane - 1, 1, 2))
    place = jnp.stack([me & 3, distance[0], distance[1], edge])
    far_tail, far_lead = ends(global_ids, g_l, ak_l, av_l, g_r, bk_r, bv_r)
    first = along(far_tail, [(plane - 1, 0)])
    final = along(far_lead, [(0, plane - 1)])
    quarters = choose(global_ids, place, g, g_r, g_o, g_l)
    pieces = spread(quarters, me, owners)

    state = near(
        global_ids,
        rand_pick,
        place,
        queries,
        keys,
        values,
        (low, high, first, final),
        (g_r, ak_r, bk_r, av_r, bv_r),
        (g_l, ak_l, bk_l, av_l, bv_l),
    )
    weights, share, acc = score(
        global_ids, rand_pick, place, queries, pieces, (g_o, ak_o, bk_o), state
    )
    av_o = pltpu.with_memory_space_constraint(av_o, pltpu.VMEM)
    bv_o = pltpu.with_memory_space_constraint(bv_o, pltpu.VMEM)
    return last(global_ids, rand_pick, (g_o, av_o, bv_o), weights, share, acc, queries)


def solution(mesh):
    return jax.shard_map(
        whole,
        mesh=mesh,
        in_specs=(
            P(("blk", "sub"), None),
            P(("blk", "sub"), None),
            P(("blk", "sub"), None),
            P(),
            P(("blk", "sub"), None),
        ),
        out_specs=P(("blk", "sub"), None),
        check_vma=False,
    )
```

```python
import functools
import math

import jax
import jax.numpy as jnp
from jax import lax
from jax.experimental import pallas as pl
from jax.experimental.pallas import tpu as pltpu
from jax.sharding import PartitionSpec as P


H = 4
DH = 128
BS = 128
QB = 16
W = H * DH
SCALE_LOG2 = math.log2(math.e) / math.sqrt(DH)
G_N, A_N, B_N = 2, 6, 8
NEAR_VMEM, SCORE_VMEM, LAST_VMEM = 24 << 20, 24 << 20, 12 << 20
WINDOW_VMEM = 41 << 20
SMALL_VMEM = 8 << 20
HIDE = -1e30
ANY = pl.BlockSpec(memory_space=pl.ANY)
VM = pl.BlockSpec(memory_space=pltpu.VMEM)
SM = pl.BlockSpec(memory_space=pltpu.SMEM)
HB = pl.BlockSpec(memory_space=pltpu.HBM)


def first_two(gids, blocks):
    p0 = blocks - 1 - lax.rem(gids[0], blocks)
    p1 = blocks - 1 - lax.rem(gids[1], blocks)
    p1 = jnp.where(p1 == p0, lax.rem(p0 + 1, blocks), p1)
    return p0, p1, jnp.minimum(p0, p1), jnp.maximum(p0, p1)


def block_at(position, places, blocks):
    p0, p1, low, high = places
    if position == 0:
        return blocks - 1 - p0
    if position == 1:
        return blocks - 1 - p1
    k = position - 2
    k = k + (k >= low).astype(jnp.int32)
    return blocks - 1 - (k + (k >= high).astype(jnp.int32))


def position_of(block, places, blocks):
    p0, p1, low, high = places
    label = blocks - 1 - block
    rest = label - (label > low).astype(jnp.int32) - (label > high).astype(jnp.int32) + 2
    return jnp.where(label == p0, 0, jnp.where(label == p1, 1, rest))


def pack_kernel(start, count, joined, ends, gids, keys, values, *refs):
    blocks = keys.shape[0]
    places = first_two(gids, blocks)
    outs, (buf, in_sem, out_sem) = refs[:-3], refs[-3:]
    if joined:
        buf = outs[0]
    wanted = [block_at(start + i, places, blocks) for i in range(count)]
    if ends:
        wanted += [blocks - 1, 0]
    loads, stores = [], []
    for half, ref in enumerate((keys, values)):
        for i, block in enumerate(wanted):
            copy = pltpu.make_async_copy(ref.at[block], buf.at[half, i], in_sem.at[half, i])
            copy.start()
            loads.append((half, i, copy))
    for half, i, load in loads:
        load.wait()
        if joined:
            continue
        target = outs[half].at[i] if i < count else outs[2 + i - count].at[half]
        copy = pltpu.make_async_copy(buf.at[half, i], target, out_sem.at[half, i])
        copy.start()
        stores.append(copy)
    for copy in stores:
        copy.wait()


def pack(gids, keys, values, start, count, joined=False, ends=False):
    shapes = [jax.ShapeDtypeStruct((count, BS, W), keys.dtype)] * 2
    if joined:
        shapes = [jax.ShapeDtypeStruct((2, count, BS, W), keys.dtype)]
    if ends:
        shapes += [jax.ShapeDtypeStruct((2, BS, W), keys.dtype)] * 2
    places = count + 2 * ends
    return pl.pallas_call(
        functools.partial(pack_kernel, start, count, joined, ends),
        out_shape=shapes,
        in_specs=[SM, HB, HB],
        out_specs=[VM if joined else ANY] * len(shapes),
        scratch_shapes=[
            pltpu.VMEM((2, 1 if joined else places, BS, W), keys.dtype),
            pltpu.SemaphoreType.DMA((2, places)),
            pltpu.SemaphoreType.DMA((2, places)),
        ],
        compiler_params=pltpu.CompilerParams(vmem_limit_bytes=56 << 20),
        cost_estimate=pl.CostEstimate(
            flops=0, transcendentals=0, bytes_accessed=places * 4 * BS * W * 2
        ),
        name="pack",
    )(gids, keys, values)


def dot_t(a, b):
    return lax.dot_general(a, b, (((1,), (1,)), ((), ())), preferred_element_type=jnp.float32)


def dot(a, b):
    return lax.dot_general(a, b, (((1,), (0,)), ((), ())), preferred_element_type=jnp.float32)


def head(h):
    return slice(h * DH, (h + 1) * DH)


def wide(column):
    return jnp.broadcast_to(column, (BS, DH))


def ones(rows):
    return jnp.ones((rows, DH), jnp.bfloat16)


def top_of(scores, old=None):
    tops = [jnp.max(s, axis=1, keepdims=True) for s in scores]
    top = wide(functools.reduce(jnp.maximum, tops))
    return top if old is None else jnp.maximum(top, old)


def weigh(s, top):
    parts = [
        jnp.exp2((s[:, n : n + DH] - top) * SCALE_LOG2) for n in range(0, s.shape[1], DH)
    ]
    return jnp.concatenate(parts, axis=1).astype(jnp.bfloat16)


def mix(w, v):
    return dot(w, jnp.concatenate([v, ones(v.shape[0])], axis=1))


def state_of(blocks):
    return [pltpu.VMEM((blocks, H, BS, DH), jnp.float32)] * 3


def fetch_pick(position, parts, dst, sem):
    at = 0
    for part in parts:
        count = part.shape[0]

        @pl.when((position >= at) & (position < at + count))
        def _(part=part, at=at, count=count):
            pltpu.make_async_copy(part.at[jnp.clip(position - at, 0, count - 1)], dst, sem).start()

        at += count


def window_kernel(blocks, place, picks, queries, keys, values, low, high, top_ref, total_ref, acc_ref, qbuf, kbuf, vbuf, sem):
    copies = [pltpu.make_async_copy(queries, qbuf, sem.at[0, 3])]
    for half, (ref, dst) in enumerate(((keys, kbuf), (values, vbuf))):
        copies.append(pltpu.make_async_copy(ref, dst.at[pl.ds(BS, blocks * BS)], sem.at[half, 0]))
        copies.append(pltpu.make_async_copy(low.at[half], dst.at[pl.ds(0, BS)], sem.at[half, 1]))
        copies.append(
            pltpu.make_async_copy(high.at[half], dst.at[pl.ds((blocks + 1) * BS, BS)], sem.at[half, 2])
        )
    for copy in copies:
        copy.start()
    for copy in copies:
        copy.wait()

    def step(j, carry):
        rows = pl.ds(pl.multiple_of(j * BS, BS), BS)
        span = pl.ds(pl.multiple_of(j * BS, BS), 3 * BS)
        no_low = jnp.where((place[3] == 0) & (j == 0), HIDE, 0.0)
        no_high = jnp.where((place[3] == 1) & (j == blocks - 1), HIDE, 0.0)
        q = [qbuf[rows, head(h)] for h in range(H)]
        k = [kbuf[span, head(h)] for h in range(H)]
        v = [vbuf[span, head(h)] for h in range(H)]
        scores = []
        for h in range(H):
            s = dot_t(q[h], k[h])
            scores.append(
                jnp.concatenate(
                    [s[:, :BS] + no_low, s[:, BS : 2 * BS], s[:, 2 * BS :] + no_high], axis=1
                )
            )
        tops = [top_of([scores[h]]) for h in range(H)]
        weights = [weigh(scores[h], tops[h]) for h in range(H)]
        mixed = [mix(weights[h], v[h]) for h in range(H)]
        for h in range(H):
            top_ref[j, h] = tops[h]
            total_ref[j, h] = mixed[h][:, DH:]
            acc_ref[j, h] = mixed[h][:, :DH]
        return carry

    lax.fori_loop(0, blocks, step, 0)


def window(place, picks, queries, keys, values, low, high):
    rows = queries.shape[0]
    blocks = rows // BS
    return pl.pallas_call(
        functools.partial(window_kernel, blocks),
        out_shape=state_of(blocks),
        in_specs=[SM, SM] + [ANY] * 5,
        out_specs=[VM] * 3,
        scratch_shapes=[
            pltpu.VMEM((rows, W), keys.dtype),
            pltpu.VMEM(((blocks + 2) * BS, W), keys.dtype),
            pltpu.VMEM(((blocks + 2) * BS, W), keys.dtype),
            pltpu.SemaphoreType.DMA((2, 4)),
        ],
        compiler_params=pltpu.CompilerParams(vmem_limit_bytes=WINDOW_VMEM),
        cost_estimate=pl.CostEstimate(
            flops=rows * 3 * BS * W * 4, transcendentals=rows * 3 * BS * H, bytes_accessed=20 << 20
        ),
        name="window",
    )(place, picks, queries, keys, values, low, high)


def near_kernel(blocks, gids, picks, place, queries, first, last, *refs):
    sides, refs = (refs[:5], refs[5:10]), refs[10:]
    top_in, total_in, acc_in, top_ref, total_ref, acc_ref, qbuf, wrap, buf, sem, pick_sem = refs
    places = first_two(gids, blocks)
    copies = [
        pltpu.make_async_copy(queries, qbuf, sem.at[0]),
        pltpu.make_async_copy(first, wrap.at[0], sem.at[1]),
        pltpu.make_async_copy(last, wrap.at[1], sem.at[2]),
    ]
    for copy in copies:
        copy.start()

    def fetch(j, carry):
        for side, column in ((0, 0), (1, 2)):
            g, a_k, b_k, a_v, b_v = sides[side]
            position = position_of(picks[j, column], places, blocks)
            fetch_pick(position, (g.at[0], a_k, b_k), buf.at[j, 0, side], pick_sem.at[j, 0, side])
            fetch_pick(position, (g.at[1], a_v, b_v), buf.at[j, 1, side], pick_sem.at[j, 1, side])
        return carry

    lax.fori_loop(0, blocks, fetch, 0)
    for copy in copies:
        copy.wait()

    def update(j, keys_of, values_of, source):
        rows = pl.ds(pl.multiple_of(j * BS, BS), BS)
        tops_in, totals_in, accs_in = source
        q = [qbuf[rows, head(h)] for h in range(H)]
        old_top = [tops_in[j, h] for h in range(H)]
        old_total = [totals_in[j, h] for h in range(H)]
        old_acc = [accs_in[j, h] for h in range(H)]
        scores = [dot_t(q[h], keys_of[h]) for h in range(H)]
        tops = [top_of([scores[h]], old_top[h]) for h in range(H)]
        weights = [weigh(scores[h], tops[h]) for h in range(H)]
        mixed = [mix(weights[h], values_of[h]) for h in range(H)]
        fades = [jnp.exp2((old_top[h] - tops[h]) * SCALE_LOG2) for h in range(H)]
        for h in range(H):
            top_ref[j, h] = tops[h]
            total_ref[j, h] = mixed[h][:, DH:] + fades[h] * old_total[h]
            acc_ref[j, h] = mixed[h][:, :DH] + fades[h] * old_acc[h]

    def step(j, carry):
        for half in range(2):
            for side in range(2):
                pltpu.make_async_copy(
                    sides[side][2].at[0], buf.at[j, half, side], pick_sem.at[j, half, side]
                ).wait()
        keys_of, values_of = [
            [
                jnp.concatenate([buf[j, half, side, :, head(h)] for side in range(2)], axis=0)
                for h in range(H)
            ]
            for half in range(2)
        ]
        update(j, keys_of, values_of, (top_in, total_in, acc_in))
        return carry

    lax.fori_loop(0, blocks, step, 0)

    @pl.when(place[3] < 2)
    def _():
        edge = jnp.where(place[3] == 0, 0, 1)
        update(
            jnp.where(place[3] == 0, 0, blocks - 1),
            [wrap[edge, 0, :, head(h)] for h in range(H)],
            [wrap[edge, 1, :, head(h)] for h in range(H)],
            (top_ref, total_ref, acc_ref),
        )


def near(gids, picks, place, queries, first, last, from_right, from_left, state):
    rows = queries.shape[0]
    blocks = rows // BS
    return pl.pallas_call(
        functools.partial(near_kernel, blocks),
        out_shape=state_of(blocks),
        in_specs=[SM, SM, SM] + [ANY] * 13 + [VM] * 3,
        out_specs=[VM] * 3,
        input_output_aliases={16: 0, 17: 1, 18: 2},
        scratch_shapes=[
            pltpu.VMEM((rows, W), queries.dtype),
            pltpu.VMEM((2, 2, BS, W), queries.dtype),
            pltpu.VMEM((blocks, 2, 2, BS, W), queries.dtype),
            pltpu.SemaphoreType.DMA((3,)),
            pltpu.SemaphoreType.DMA((blocks, 2, 2)),
        ],
        compiler_params=pltpu.CompilerParams(vmem_limit_bytes=NEAR_VMEM),
        cost_estimate=pl.CostEstimate(
            flops=rows * 2 * BS * W * 4, transcendentals=rows * 2 * BS * H, bytes_accessed=30 << 20
        ),
        name="near",
    )(gids, picks, place, queries, first, last, *from_right, *from_left, *state)


def score_kernel(blocks, gids, picks, place, q_ref, *refs):
    pieces, (g_o, ak_o, bk_o), refs = refs[:4], refs[4:7], refs[7:]
    top_in, total_in, acc_in, weight_ref, share_ref, acc_ref, shared, buf, shared_sem, sem = refs
    places = first_two(gids, blocks)
    copies = []
    for n, piece in enumerate(pieces):
        quarter = jnp.bitwise_and(jnp.bitwise_xor(place[0], n), 3)
        rows = piece.shape[1]
        start = jnp.bitwise_and(quarter, 1) * (2 * rows) + jnp.right_shift(quarter, 1) * rows
        at = pl.ds(pl.multiple_of(start, rows), rows)
        copies.append(pltpu.make_async_copy(piece, shared.at[:, at], shared_sem.at[n]))
    for copy in copies:
        copy.start()

    def fetch(j, carry):
        position = position_of(picks[j, 1], places, blocks)
        fetch_pick(position, (g_o.at[0], ak_o, bk_o), buf.at[j], sem.at[j])
        return carry

    lax.fori_loop(0, blocks, fetch, 0)
    for copy in copies:
        copy.wait()

    def step(j, carry):
        rows = pl.ds(pl.multiple_of(j * BS, BS), BS)
        pltpu.make_async_copy(bk_o.at[0], buf.at[j], sem.at[j]).wait()
        q = [q_ref[rows, head(h)] for h in range(H)]
        k = [
            jnp.concatenate(
                [shared[0, :BS, head(h)], shared[1, :BS, head(h)], buf[j, :, head(h)]], axis=0
            )
            for h in range(H)
        ]
        v = [jnp.concatenate([shared[n, BS:, head(h)] for n in range(2)], axis=0) for h in range(H)]
        old_top = [top_in[j, h] for h in range(H)]
        old_total = [total_in[j, h] for h in range(H)]
        old_acc = [acc_in[j, h] for h in range(H)]
        scores = [dot_t(q[h], k[h]) for h in range(H)]
        tops = [top_of([scores[h]], old_top[h]) for h in range(H)]
        weights = [weigh(scores[h], tops[h]) for h in range(H)]
        mixed = [mix(weights[h][:, : 2 * BS], v[h]) for h in range(H)]
        sums = [mixed[h][:, DH:] + dot(weights[h][:, 2 * BS :], ones(BS)) for h in range(H)]
        fades = [jnp.exp2((old_top[h] - tops[h]) * SCALE_LOG2) for h in range(H)]
        shares = [1.0 / (sums[h] + fades[h] * old_total[h]) for h in range(H)]
        for h in range(H):
            weight_ref[j, h] = weights[h][:, 2 * BS :]
            share_ref[j, h] = shares[h]
            acc_ref[j, h] = mixed[h][:, :DH] + old_acc[h] * fades[h]
        return carry

    lax.fori_loop(0, blocks, step, 0)


def score(gids, picks, place, queries, pieces, opposite, state):
    rows = queries.shape[0]
    blocks = rows // BS
    floats = jax.ShapeDtypeStruct((blocks, H, BS, DH), jnp.float32)
    return pl.pallas_call(
        functools.partial(score_kernel, blocks),
        out_shape=[jax.ShapeDtypeStruct((blocks, H, BS, BS), queries.dtype), floats, floats],
        in_specs=[SM, SM, SM, VM] + [ANY] * 7 + [VM] * 3,
        out_specs=[VM] * 3,
        input_output_aliases={12: 1, 13: 2},
        scratch_shapes=[
            pltpu.VMEM((2, 2 * BS, W), queries.dtype),
            pltpu.VMEM((blocks, BS, W), queries.dtype),
            pltpu.SemaphoreType.DMA((4,)),
            pltpu.SemaphoreType.DMA((blocks,)),
        ],
        compiler_params=pltpu.CompilerParams(vmem_limit_bytes=SCORE_VMEM),
        cost_estimate=pl.CostEstimate(
            flops=rows * BS * W * 10, transcendentals=rows * 3 * BS * H, bytes_accessed=28 << 20
        ),
        name="score",
    )(gids, picks, place, queries, *pieces, *opposite, *state)


def last_kernel(blocks, gids, picks, g, a_v, b_v, weights, share, acc, out, obuf, out_sem):
    places = first_two(gids, blocks)

    def store(j):
        rows = pl.ds(pl.multiple_of(j * BS, BS), BS)
        return pltpu.make_async_copy(obuf.at[j], out.at[rows], out_sem.at[j])

    def step(j, carry):
        position = position_of(picks[j, 1], places, blocks)

        def finish(v):
            mixed = [(dot(weights[j, h], v[:, head(h)]) + acc[j, h]) * share[j, h] for h in range(H)]
            for h in range(H):
                obuf[j, :, head(h)] = mixed[h].astype(obuf.dtype)

        @pl.when(position < G_N)
        def _():
            finish(g.at[1, jnp.minimum(position, G_N - 1)])

        @pl.when((position >= G_N) & (position < G_N + A_N))
        def _():
            finish(a_v.at[jnp.clip(position - G_N, 0, A_N - 1)])

        @pl.when(position >= G_N + A_N)
        def _():
            finish(b_v.at[jnp.clip(position - G_N - A_N, 0, B_N - 1)])

        store(j).start()
        return carry

    lax.fori_loop(0, blocks, step, 0)

    def drain(j, carry):
        store(j).wait()
        return carry

    lax.fori_loop(0, blocks, drain, 0)


def last(gids, picks, parts, weights, share, acc, like):
    rows = like.shape[0]
    blocks = rows // BS
    return pl.pallas_call(
        functools.partial(last_kernel, blocks),
        out_shape=jax.ShapeDtypeStruct(like.shape, like.dtype),
        in_specs=[SM, SM] + [VM] * 6,
        out_specs=ANY,
        scratch_shapes=[
            pltpu.VMEM((blocks, BS, W), like.dtype),
            pltpu.SemaphoreType.DMA((blocks,)),
        ],
        compiler_params=pltpu.CompilerParams(vmem_limit_bytes=LAST_VMEM),
        cost_estimate=pl.CostEstimate(
            flops=rows * BS * W * 2, transcendentals=0, bytes_accessed=10 << 20
        ),
        name="last",
    )(gids, picks, *parts, weights, share, acc)


ALL = ("blk", "sub")


def choose_kernel(gids, place, g, g_r, g_o, g_l, keep, give_1, give_2, give_3, sem):
    blocks = QB
    rows = keep.shape[1]
    p0, p1 = lax.rem(gids[0], blocks), lax.rem(gids[1], blocks)
    slots = (0, jnp.where(p0 == p1, 0, 1))
    outs = (keep, give_1, give_2, give_3)
    for i in range(2):
        distance = lax.rem(place[i + 1] + 4, 4)
        for d, source in enumerate((g, g_r, g_o, g_l)):

            @pl.when(distance == d)
            def _(i=i, source=source):
                for n, out in enumerate(outs):
                    quarter = jnp.bitwise_xor(place[0], n)
                    half = jnp.bitwise_and(quarter, 1)
                    at = pl.ds(pl.multiple_of(jnp.right_shift(quarter, 1) * rows, rows), rows)
                    pltpu.make_async_copy(source.at[half, slots[i], at], out.at[i], sem.at[i, n]).start()

    for i in range(2):
        for n, out in enumerate(outs):
            pltpu.make_async_copy(g.at[0, 0, pl.ds(0, rows)], out.at[i], sem.at[i, n]).wait()


def choose(gids, place, g, g_r, g_o, g_l):
    piece = jax.ShapeDtypeStruct((2, BS // 2, W), g.dtype)
    return pl.pallas_call(
        choose_kernel,
        out_shape=[piece] * 4,
        in_specs=[SM, SM] + [ANY] * 4,
        out_specs=[VM] * 4,
        scratch_shapes=[pltpu.SemaphoreType.DMA((2, 4))],
        compiler_params=pltpu.CompilerParams(vmem_limit_bytes=SMALL_VMEM),
        cost_estimate=pl.CostEstimate(flops=0, transcendentals=0, bytes_accessed=1 << 20),
        name="choose",
    )(gids, place, g, g_r, g_o, g_l)


def ends_kernel(gids, g_l, ak_l, av_l, g_r, bk_r, bv_r, tail, lead, sem):
    p0, p1, _, _ = first_two(gids, QB)
    cases = (
        (0, tail, g_l, (ak_l.at[0], av_l.at[0])),
        (QB - 1, lead, g_r, (bk_r.at[B_N - 1], bv_r.at[B_N - 1])),
    )
    for n, (label, out, g, rest) in enumerate(cases):
        for half in range(2):
            done = sem.at[n, half]

            @pl.when(p0 == label)
            def _(g=g, half=half, out=out, done=done):
                pltpu.make_async_copy(g.at[half, 0], out.at[half], done).start()

            @pl.when(p1 == label)
            def _(g=g, half=half, out=out, done=done):
                pltpu.make_async_copy(g.at[half, 1], out.at[half], done).start()

            @pl.when((p0 != label) & (p1 != label))
            def _(rest=rest, half=half, out=out, done=done):
                pltpu.make_async_copy(rest[half], out.at[half], done).start()

    for n, (_, out, _, rest) in enumerate(cases):
        for half in range(2):
            pltpu.make_async_copy(rest[half], out.at[half], sem.at[n, half]).wait()


def ends(gids, g_l, ak_l, av_l, g_r, bk_r, bv_r):
    block = jax.ShapeDtypeStruct((2, BS, W), g_l.dtype)
    return pl.pallas_call(
        ends_kernel,
        out_shape=[block] * 2,
        in_specs=[SM] + [ANY] * 6,
        out_specs=[VM] * 2,
        scratch_shapes=[pltpu.SemaphoreType.DMA((2, 2))],
        compiler_params=pltpu.CompilerParams(vmem_limit_bytes=SMALL_VMEM),
        cost_estimate=pl.CostEstimate(flops=0, transcendentals=0, bytes_accessed=1 << 20),
        name="ends",
    )(gids, g_l, ak_l, av_l, g_r, bk_r, bv_r)


def swap(value, bits):
    count = lax.axis_size(ALL)
    return lax.ppermute(value, ALL, [(i, i ^ bits) for i in range(count)])


def pick_slots(mask, a, b):
    return jnp.where(mask[:, None, None], a, b)


def masks_of(me, owners):
    differ = (me ^ owners) & 3
    rows = [differ == n for n in (1, 2, 3)]
    rows += [((me >> bit) & 1) == ((owners >> bit) & 1) for bit in (2, 3, 4, 5)]
    return jnp.stack(rows).astype(jnp.int32)


def spread(quarters, masks):
    value = quarters[0]
    given = [swap(quarters[n], n) for n in (1, 2, 3)]
    for n in (1, 2, 3):
        value = pick_slots(masks[n - 1] == 1, given[n - 1], value)
    for bit in (2, 3, 4, 5):
        value = pick_slots(masks[bit + 1] == 1, value, swap(value, 1 << bit))
    return [value] + [swap(value, n) for n in (1, 2, 3)]


def whole(queries, keys, values, global_ids, rand_pick):
    rows, width = queries.shape
    blocks = rows // BS
    count = lax.axis_size("blk")
    quarter = count // 4
    right = [(i, (i + quarter) % count) for i in range(count)]
    left = [(i, (i - quarter) % count) for i in range(count)]
    everyone = lax.axis_size(ALL)

    def to_right(v):
        return lax.ppermute(v, "blk", right)

    def to_left(v):
        return lax.ppermute(v, "blk", left)

    plane = everyone // 4

    def along(v, pairs):
        return lax.ppermute(
            v, ALL, [(p * plane + i, p * plane + j) for p in range(4) for i, j in pairs]
        )

    key_blocks = keys.reshape(blocks, BS, width)
    value_blocks = values.reshape(blocks, BS, width)
    (g,) = pack(global_ids, key_blocks, value_blocks, 0, G_N, joined=True)
    g_l, g_r = to_right(g), to_left(g)
    ak, av, tail, lead = pack(global_ids, key_blocks, value_blocks, G_N, A_N, ends=True)
    bk, bv = pack(global_ids, key_blocks, value_blocks, G_N + A_N, B_N)
    ak_l, av_l = to_right(ak), to_right(av)
    bk_r, bv_r = to_left(bk), to_left(bv)
    low = along(tail, [(i, i + 1) for i in range(plane - 1)])
    high = along(lead, [(i + 1, i) for i in range(plane - 1)])
    g_o = to_right(g_l)
    bk_l, bv_l = to_right(bk), to_right(bv)
    ak_r, av_r = to_left(ak), to_left(av)
    ak_o, bk_o = to_right(ak_l), to_left(bk_r)
    av_o, bv_o = to_right(av_l), to_left(bv_r)

    me = lax.axis_index(ALL)
    owners = global_ids // blocks
    distance = owners // plane - me // plane
    spot = me % plane
    edge = jnp.where(spot == 0, 0, jnp.where(spot == plane - 1, 1, 2))
    place = jnp.stack([me & 3, distance[0], distance[1], edge])
    place, masks = lax.optimization_barrier((place, masks_of(me, owners)))
    state = window(place, rand_pick, queries, keys, values, low, high)
    far_tail, far_lead = ends(global_ids, g_l, ak_l, av_l, g_r, bk_r, bv_r)
    first = along(far_tail, [(plane - 1, 0)])
    final = along(far_lead, [(0, plane - 1)])
    quarters = choose(global_ids, place, g, g_r, g_o, g_l)
    pieces = spread(quarters, masks)

    state = near(
        global_ids,
        rand_pick,
        place,
        queries,
        first,
        final,
        (g_r, ak_r, bk_r, av_r, bv_r),
        (g_l, ak_l, bk_l, av_l, bv_l),
        state,
    )
    weights, share, acc = score(
        global_ids, rand_pick, place, queries, pieces, (g_o, ak_o, bk_o), state
    )
    av_o = pltpu.with_memory_space_constraint(av_o, pltpu.VMEM)
    bv_o = pltpu.with_memory_space_constraint(bv_o, pltpu.VMEM)
    return last(global_ids, rand_pick, (g_o, av_o, bv_o), weights, share, acc, queries)


def solution(mesh):
    return jax.shard_map(
        whole,
        mesh=mesh,
        in_specs=(
            P(("blk", "sub"), None),
            P(("blk", "sub"), None),
            P(("blk", "sub"), None),
            P(),
            P(("blk", "sub"), None),
        ),
        out_specs=P(("blk", "sub"), None),
        check_vma=False,
    )
```

```python
import functools
import math

import jax
import jax.numpy as jnp
from jax import lax
from jax.experimental import pallas as pl
from jax.experimental.pallas import tpu as pltpu
from jax.sharding import PartitionSpec as P


H = 4
DH = 128
BS = 128
QB = 16
W = H * DH
SCALE_LOG2 = math.log2(math.e) / math.sqrt(DH)
G_N, A_N, B_N = 2, 6, 8
NEAR_VMEM, SCORE_VMEM, LAST_VMEM = 24 << 20, 24 << 20, 12 << 20
WINDOW_VMEM = 41 << 20
SMALL_VMEM = 8 << 20
HIDE = -1e30
ANY = pl.BlockSpec(memory_space=pl.ANY)
VM = pl.BlockSpec(memory_space=pltpu.VMEM)
SM = pl.BlockSpec(memory_space=pltpu.SMEM)
HB = pl.BlockSpec(memory_space=pltpu.HBM)


def first_two(gids, blocks):
    p0 = blocks - 1 - lax.rem(gids[0], blocks)
    p1 = blocks - 1 - lax.rem(gids[1], blocks)
    p1 = jnp.where(p1 == p0, lax.rem(p0 + 1, blocks), p1)
    return p0, p1, jnp.minimum(p0, p1), jnp.maximum(p0, p1)


def block_at(position, places, blocks):
    p0, p1, low, high = places
    if position == 0:
        return blocks - 1 - p0
    if position == 1:
        return blocks - 1 - p1
    k = position - 2
    k = k + (k >= low).astype(jnp.int32)
    return blocks - 1 - (k + (k >= high).astype(jnp.int32))


def position_of(block, places, blocks):
    p0, p1, low, high = places
    label = blocks - 1 - block
    rest = label - (label > low).astype(jnp.int32) - (label > high).astype(jnp.int32) + 2
    return jnp.where(label == p0, 0, jnp.where(label == p1, 1, rest))


def pack_kernel(start, count, joined, ends, gids, keys, values, *refs):
    blocks = keys.shape[0]
    places = first_two(gids, blocks)
    outs, (buf, in_sem, out_sem) = refs[:-3], refs[-3:]
    if joined:
        buf = outs[0]
    wanted = [block_at(start + i, places, blocks) for i in range(count)]
    if ends:
        wanted += [blocks - 1, 0]
    loads, stores = [], []
    for half, ref in enumerate((keys, values)):
        for i, block in enumerate(wanted):
            copy = pltpu.make_async_copy(ref.at[block], buf.at[half, i], in_sem.at[half, i])
            copy.start()
            loads.append((half, i, copy))
    for half, i, load in loads:
        load.wait()
        if joined:
            continue
        target = outs[half].at[i] if i < count else outs[2 + i - count].at[half]
        copy = pltpu.make_async_copy(buf.at[half, i], target, out_sem.at[half, i])
        copy.start()
        stores.append(copy)
    for copy in stores:
        copy.wait()


def pack(gids, keys, values, start, count, joined=False, ends=False):
    shapes = [jax.ShapeDtypeStruct((count, BS, W), keys.dtype)] * 2
    if joined:
        shapes = [pltpu.VMEM((2, count, BS, W), keys.dtype)]
    if ends:
        shapes += [jax.ShapeDtypeStruct((2, BS, W), keys.dtype)] * 2
    places = count + 2 * ends
    return pl.pallas_call(
        functools.partial(pack_kernel, start, count, joined, ends),
        out_shape=shapes,
        in_specs=[SM, HB, HB],
        out_specs=[VM if joined else ANY] * len(shapes),
        scratch_shapes=[
            pltpu.VMEM((2, 1 if joined else places, BS, W), keys.dtype),
            pltpu.SemaphoreType.DMA((2, places)),
            pltpu.SemaphoreType.DMA((2, places)),
        ],
        compiler_params=pltpu.CompilerParams(vmem_limit_bytes=56 << 20),
        cost_estimate=pl.CostEstimate(
            flops=0, transcendentals=0, bytes_accessed=places * 4 * BS * W * 2
        ),
        name="pack",
    )(gids, keys, values)


def dot_t(a, b):
    return lax.dot_general(a, b, (((1,), (1,)), ((), ())), preferred_element_type=jnp.float32)


def dot(a, b):
    return lax.dot_general(a, b, (((1,), (0,)), ((), ())), preferred_element_type=jnp.float32)


def head(h):
    return slice(h * DH, (h + 1) * DH)


def wide(column):
    return jnp.broadcast_to(column, (BS, DH))


def ones(rows):
    return jnp.ones((rows, DH), jnp.bfloat16)


def top_of(scores, old=None):
    tops = [jnp.max(s, axis=1, keepdims=True) for s in scores]
    top = wide(functools.reduce(jnp.maximum, tops))
    return top if old is None else jnp.maximum(top, old)


def weigh(s, top):
    parts = [
        jnp.exp2((s[:, n : n + DH] - top) * SCALE_LOG2) for n in range(0, s.shape[1], DH)
    ]
    return jnp.concatenate(parts, axis=1).astype(jnp.bfloat16)


def mix(w, v):
    return dot(w, jnp.concatenate([v, ones(v.shape[0])], axis=1))


def state_of(blocks):
    return [pltpu.VMEM((blocks, H, BS, DH), jnp.float32)] * 3


def fetch_pick(position, parts, dst, sem):
    at = 0
    for part in parts:
        count = part.shape[0]

        @pl.when((position >= at) & (position < at + count))
        def _(part=part, at=at, count=count):
            pltpu.make_async_copy(part.at[jnp.clip(position - at, 0, count - 1)], dst, sem).start()

        at += count


def window_kernel(blocks, place, picks, queries, keys, values, low, high, top_ref, total_ref, acc_ref, qbuf, kbuf, vbuf, sem):
    copies = [pltpu.make_async_copy(queries, qbuf, sem.at[0, 3])]
    for half, (ref, dst) in enumerate(((keys, kbuf), (values, vbuf))):
        copies.append(pltpu.make_async_copy(ref, dst.at[pl.ds(BS, blocks * BS)], sem.at[half, 0]))
        copies.append(pltpu.make_async_copy(low.at[half], dst.at[pl.ds(0, BS)], sem.at[half, 1]))
        copies.append(
            pltpu.make_async_copy(high.at[half], dst.at[pl.ds((blocks + 1) * BS, BS)], sem.at[half, 2])
        )
    for copy in copies:
        copy.start()
    for copy in copies:
        copy.wait()

    def step(j, carry):
        rows = pl.ds(pl.multiple_of(j * BS, BS), BS)
        span = pl.ds(pl.multiple_of(j * BS, BS), 3 * BS)
        no_low = jnp.where((place[3] == 0) & (j == 0), HIDE, 0.0)
        no_high = jnp.where((place[3] == 1) & (j == blocks - 1), HIDE, 0.0)
        q = [qbuf[rows, head(h)] for h in range(H)]
        k = [kbuf[span, head(h)] for h in range(H)]
        v = [vbuf[span, head(h)] for h in range(H)]
        scores = []
        for h in range(H):
            s = dot_t(q[h], k[h])
            scores.append(
                jnp.concatenate(
                    [s[:, :BS] + no_low, s[:, BS : 2 * BS], s[:, 2 * BS :] + no_high], axis=1
                )
            )
        tops = [top_of([scores[h]]) for h in range(H)]
        weights = [weigh(scores[h], tops[h]) for h in range(H)]
        mixed = [mix(weights[h], v[h]) for h in range(H)]
        for h in range(H):
            top_ref[j, h] = tops[h]
            total_ref[j, h] = mixed[h][:, DH:]
            acc_ref[j, h] = mixed[h][:, :DH]
        return carry

    lax.fori_loop(0, blocks, step, 0)


def window(place, picks, queries, keys, values, low, high):
    rows = queries.shape[0]
    blocks = rows // BS
    return pl.pallas_call(
        functools.partial(window_kernel, blocks),
        out_shape=state_of(blocks),
        in_specs=[SM, SM] + [ANY] * 5,
        out_specs=[VM] * 3,
        scratch_shapes=[
            pltpu.VMEM((rows, W), keys.dtype),
            pltpu.VMEM(((blocks + 2) * BS, W), keys.dtype),
            pltpu.VMEM(((blocks + 2) * BS, W), keys.dtype),
            pltpu.SemaphoreType.DMA((2, 4)),
        ],
        compiler_params=pltpu.CompilerParams(vmem_limit_bytes=WINDOW_VMEM),
        cost_estimate=pl.CostEstimate(
            flops=rows * 3 * BS * W * 4, transcendentals=rows * 3 * BS * H, bytes_accessed=20 << 20
        ),
        name="window",
    )(place, picks, queries, keys, values, low, high)


def near_kernel(blocks, gids, picks, place, queries, first, last, *refs):
    sides, refs = (refs[:5], refs[5:10]), refs[10:]
    top_in, total_in, acc_in, top_ref, total_ref, acc_ref, qbuf, wrap, buf, sem, pick_sem = refs
    places = first_two(gids, blocks)
    copies = [
        pltpu.make_async_copy(queries, qbuf, sem.at[0]),
        pltpu.make_async_copy(first, wrap.at[0], sem.at[1]),
        pltpu.make_async_copy(last, wrap.at[1], sem.at[2]),
    ]
    for copy in copies:
        copy.start()

    def fetch(j, carry):
        for side, column in ((0, 0), (1, 2)):
            g, a_k, b_k, a_v, b_v = sides[side]
            position = position_of(picks[j, column], places, blocks)
            fetch_pick(position, (g.at[0], a_k, b_k), buf.at[j, 0, side], pick_sem.at[j, 0, side])
            fetch_pick(position, (g.at[1], a_v, b_v), buf.at[j, 1, side], pick_sem.at[j, 1, side])
        return carry

    lax.fori_loop(0, blocks, fetch, 0)
    for copy in copies:
        copy.wait()

    def update(j, keys_of, values_of, source):
        rows = pl.ds(pl.multiple_of(j * BS, BS), BS)
        tops_in, totals_in, accs_in = source
        q = [qbuf[rows, head(h)] for h in range(H)]
        old_top = [tops_in[j, h] for h in range(H)]
        old_total = [totals_in[j, h] for h in range(H)]
        old_acc = [accs_in[j, h] for h in range(H)]
        scores = [dot_t(q[h], keys_of[h]) for h in range(H)]
        tops = [top_of([scores[h]], old_top[h]) for h in range(H)]
        weights = [weigh(scores[h], tops[h]) for h in range(H)]
        mixed = [mix(weights[h], values_of[h]) for h in range(H)]
        fades = [jnp.exp2((old_top[h] - tops[h]) * SCALE_LOG2) for h in range(H)]
        for h in range(H):
            top_ref[j, h] = tops[h]
            total_ref[j, h] = mixed[h][:, DH:] + fades[h] * old_total[h]
            acc_ref[j, h] = mixed[h][:, :DH] + fades[h] * old_acc[h]

    def step(j, carry):
        for half in range(2):
            for side in range(2):
                pltpu.make_async_copy(
                    sides[side][2].at[0], buf.at[j, half, side], pick_sem.at[j, half, side]
                ).wait()
        keys_of, values_of = [
            [
                jnp.concatenate([buf[j, half, side, :, head(h)] for side in range(2)], axis=0)
                for h in range(H)
            ]
            for half in range(2)
        ]
        update(j, keys_of, values_of, (top_in, total_in, acc_in))
        return carry

    lax.fori_loop(0, blocks, step, 0)

    @pl.when(place[3] < 2)
    def _():
        edge = jnp.where(place[3] == 0, 0, 1)
        update(
            jnp.where(place[3] == 0, 0, blocks - 1),
            [wrap[edge, 0, :, head(h)] for h in range(H)],
            [wrap[edge, 1, :, head(h)] for h in range(H)],
            (top_ref, total_ref, acc_ref),
        )


def near(gids, picks, place, queries, first, last, from_right, from_left, state):
    rows = queries.shape[0]
    blocks = rows // BS
    return pl.pallas_call(
        functools.partial(near_kernel, blocks),
        out_shape=state_of(blocks),
        in_specs=[SM, SM, SM] + [ANY] * 13 + [VM] * 3,
        out_specs=[VM] * 3,
        input_output_aliases={16: 0, 17: 1, 18: 2},
        scratch_shapes=[
            pltpu.VMEM((rows, W), queries.dtype),
            pltpu.VMEM((2, 2, BS, W), queries.dtype),
            pltpu.VMEM((blocks, 2, 2, BS, W), queries.dtype),
            pltpu.SemaphoreType.DMA((3,)),
            pltpu.SemaphoreType.DMA((blocks, 2, 2)),
        ],
        compiler_params=pltpu.CompilerParams(vmem_limit_bytes=NEAR_VMEM),
        cost_estimate=pl.CostEstimate(
            flops=rows * 2 * BS * W * 4, transcendentals=rows * 2 * BS * H, bytes_accessed=30 << 20
        ),
        name="near",
    )(gids, picks, place, queries, first, last, *from_right, *from_left, *state)


def score_kernel(blocks, gids, picks, place, q_ref, *refs):
    pieces, (g_o, ak_o, bk_o), refs = refs[:4], refs[4:7], refs[7:]
    top_in, total_in, acc_in, weight_ref, share_ref, acc_ref, shared, buf, shared_sem, sem = refs
    places = first_two(gids, blocks)
    copies = []
    for n, piece in enumerate(pieces):
        quarter = jnp.bitwise_and(jnp.bitwise_xor(place[0], n), 3)
        rows = piece.shape[1]
        start = jnp.bitwise_and(quarter, 1) * (2 * rows) + jnp.right_shift(quarter, 1) * rows
        at = pl.ds(pl.multiple_of(start, rows), rows)
        copies.append(pltpu.make_async_copy(piece, shared.at[:, at], shared_sem.at[n]))
    for copy in copies:
        copy.start()

    def fetch(j, carry):
        position = position_of(picks[j, 1], places, blocks)
        fetch_pick(position, (g_o.at[0], ak_o, bk_o), buf.at[j], sem.at[j])
        return carry

    lax.fori_loop(0, blocks, fetch, 0)
    for copy in copies:
        copy.wait()

    def step(j, carry):
        rows = pl.ds(pl.multiple_of(j * BS, BS), BS)
        pltpu.make_async_copy(bk_o.at[0], buf.at[j], sem.at[j]).wait()
        q = [q_ref[rows, head(h)] for h in range(H)]
        k = [
            jnp.concatenate(
                [shared[0, :BS, head(h)], shared[1, :BS, head(h)], buf[j, :, head(h)]], axis=0
            )
            for h in range(H)
        ]
        v = [jnp.concatenate([shared[n, BS:, head(h)] for n in range(2)], axis=0) for h in range(H)]
        old_top = [top_in[j, h] for h in range(H)]
        old_total = [total_in[j, h] for h in range(H)]
        old_acc = [acc_in[j, h] for h in range(H)]
        scores = [dot_t(q[h], k[h]) for h in range(H)]
        tops = [top_of([scores[h]], old_top[h]) for h in range(H)]
        weights = [weigh(scores[h], tops[h]) for h in range(H)]
        mixed = [mix(weights[h][:, : 2 * BS], v[h]) for h in range(H)]
        sums = [mixed[h][:, DH:] + dot(weights[h][:, 2 * BS :], ones(BS)) for h in range(H)]
        fades = [jnp.exp2((old_top[h] - tops[h]) * SCALE_LOG2) for h in range(H)]
        shares = [1.0 / (sums[h] + fades[h] * old_total[h]) for h in range(H)]
        for h in range(H):
            weight_ref[j, h] = weights[h][:, 2 * BS :]
            share_ref[j, h] = shares[h]
            acc_ref[j, h] = mixed[h][:, :DH] + old_acc[h] * fades[h]
        return carry

    lax.fori_loop(0, blocks, step, 0)


def score(gids, picks, place, queries, pieces, opposite, state):
    rows = queries.shape[0]
    blocks = rows // BS
    floats = jax.ShapeDtypeStruct((blocks, H, BS, DH), jnp.float32)
    return pl.pallas_call(
        functools.partial(score_kernel, blocks),
        out_shape=[jax.ShapeDtypeStruct((blocks, H, BS, BS), queries.dtype), floats, floats],
        in_specs=[SM, SM, SM, VM] + [ANY] * 7 + [VM] * 3,
        out_specs=[VM] * 3,
        input_output_aliases={12: 1, 13: 2},
        scratch_shapes=[
            pltpu.VMEM((2, 2 * BS, W), queries.dtype),
            pltpu.VMEM((blocks, BS, W), queries.dtype),
            pltpu.SemaphoreType.DMA((4,)),
            pltpu.SemaphoreType.DMA((blocks,)),
        ],
        compiler_params=pltpu.CompilerParams(vmem_limit_bytes=SCORE_VMEM),
        cost_estimate=pl.CostEstimate(
            flops=rows * BS * W * 10, transcendentals=rows * 3 * BS * H, bytes_accessed=28 << 20
        ),
        name="score",
    )(gids, picks, place, queries, *pieces, *opposite, *state)


def last_kernel(blocks, gids, picks, g, a_v, b_v, weights, share, acc, out, obuf, order, out_sem):
    places = first_two(gids, blocks)

    def store(j):
        rows = pl.ds(pl.multiple_of(j * BS, BS), BS)
        return pltpu.make_async_copy(obuf.at[j], out.at[rows], out_sem.at[j])

    def sort(j, counts):
        position = position_of(picks[j, 1], places, blocks)
        kind = (position >= G_N).astype(jnp.int32) + (position >= G_N + A_N).astype(jnp.int32)
        at = jnp.where(kind == 0, counts[0], jnp.where(kind == 1, counts[1], counts[2]))
        order[kind * blocks + at] = j
        return tuple(count + (kind == n).astype(jnp.int32) for n, count in enumerate(counts))

    zero = jnp.int32(0)
    counts = lax.fori_loop(0, blocks, sort, (zero, zero, zero), unroll=True)

    for kind, (values, begin) in enumerate(((g.at[1], 0), (a_v, G_N), (b_v, G_N + A_N))):
        count = counts[kind]

        def pair(n, carry, kind=kind, values=values, begin=begin, count=count):
            both = [
                order[kind * blocks + 2 * n],
                order[kind * blocks + jnp.minimum(2 * n + 1, count - 1)],
            ]
            mixed = []
            for j in both:
                at = position_of(picks[j, 1], places, blocks) - begin
                at = jnp.clip(at, 0, values.shape[0] - 1)
                mixed.append([dot(weights[j, h], values[at, :, head(h)]) for h in range(H)])
            done = [
                [((m + acc[j, h]) * share[j, h]).astype(obuf.dtype) for h, m in enumerate(ms)]
                for j, ms in zip(both, mixed)
            ]
            for j, parts in zip(both, done):
                for h in range(H):
                    obuf[j, :, head(h)] = parts[h]
            store(both[0]).start()

            @pl.when(both[1] != both[0])
            def _():
                store(both[1]).start()

            return carry

        lax.fori_loop(0, lax.div(count + 1, 2), pair, 0)

    def drain(j, carry):
        store(j).wait()
        return carry

    lax.fori_loop(0, blocks, drain, 0, unroll=True)


def last(gids, picks, parts, weights, share, acc, like):
    rows = like.shape[0]
    blocks = rows // BS
    return pl.pallas_call(
        functools.partial(last_kernel, blocks),
        out_shape=jax.ShapeDtypeStruct(like.shape, like.dtype),
        in_specs=[SM, SM] + [VM] * 6,
        out_specs=ANY,
        scratch_shapes=[
            pltpu.VMEM((blocks, BS, W), like.dtype),
            pltpu.SMEM((3 * blocks,), jnp.int32),
            pltpu.SemaphoreType.DMA((blocks,)),
        ],
        compiler_params=pltpu.CompilerParams(vmem_limit_bytes=LAST_VMEM),
        cost_estimate=pl.CostEstimate(
            flops=rows * BS * W * 2, transcendentals=0, bytes_accessed=10 << 20
        ),
        name="last",
    )(gids, picks, *parts, weights, share, acc)


ALL = ("blk", "sub")


def choose_kernel(gids, place, g, g_r, g_o, g_l, keep, give_1, give_2, give_3, sem):
    blocks = QB
    rows = keep.shape[1]
    p0, p1 = lax.rem(gids[0], blocks), lax.rem(gids[1], blocks)
    slots = (0, jnp.where(p0 == p1, 0, 1))
    outs = (keep, give_1, give_2, give_3)
    for i in range(2):
        distance = lax.rem(place[i + 1] + 4, 4)
        for d, source in enumerate((g, g_r, g_o, g_l)):

            @pl.when(distance == d)
            def _(i=i, source=source):
                for n, out in enumerate(outs):
                    quarter = jnp.bitwise_xor(place[0], n)
                    half = jnp.bitwise_and(quarter, 1)
                    at = pl.ds(pl.multiple_of(jnp.right_shift(quarter, 1) * rows, rows), rows)
                    pltpu.make_async_copy(source.at[half, slots[i], at], out.at[i], sem.at[i, n]).start()

    for i in range(2):
        for n, out in enumerate(outs):
            pltpu.make_async_copy(g.at[0, 0, pl.ds(0, rows)], out.at[i], sem.at[i, n]).wait()


def choose(gids, place, g, g_r, g_o, g_l):
    piece = jax.ShapeDtypeStruct((2, BS // 2, W), g.dtype)
    return pl.pallas_call(
        choose_kernel,
        out_shape=[piece] * 4,
        in_specs=[SM, SM] + [ANY] * 4,
        out_specs=[VM] * 4,
        scratch_shapes=[pltpu.SemaphoreType.DMA((2, 4))],
        compiler_params=pltpu.CompilerParams(vmem_limit_bytes=SMALL_VMEM),
        cost_estimate=pl.CostEstimate(flops=0, transcendentals=0, bytes_accessed=1 << 20),
        name="choose",
    )(gids, place, g, g_r, g_o, g_l)


def ends_kernel(gids, g_l, ak_l, av_l, g_r, bk_r, bv_r, tail, lead, sem):
    p0, p1, _, _ = first_two(gids, QB)
    cases = (
        (0, tail, g_l, (ak_l.at[0], av_l.at[0])),
        (QB - 1, lead, g_r, (bk_r.at[B_N - 1], bv_r.at[B_N - 1])),
    )
    for n, (label, out, g, rest) in enumerate(cases):
        for half in range(2):
            done = sem.at[n, half]

            @pl.when(p0 == label)
            def _(g=g, half=half, out=out, done=done):
                pltpu.make_async_copy(g.at[half, 0], out.at[half], done).start()

            @pl.when(p1 == label)
            def _(g=g, half=half, out=out, done=done):
                pltpu.make_async_copy(g.at[half, 1], out.at[half], done).start()

            @pl.when((p0 != label) & (p1 != label))
            def _(rest=rest, half=half, out=out, done=done):
                pltpu.make_async_copy(rest[half], out.at[half], done).start()

    for n, (_, out, _, rest) in enumerate(cases):
        for half in range(2):
            pltpu.make_async_copy(rest[half], out.at[half], sem.at[n, half]).wait()


def ends(gids, g_l, ak_l, av_l, g_r, bk_r, bv_r):
    block = jax.ShapeDtypeStruct((2, BS, W), g_l.dtype)
    return pl.pallas_call(
        ends_kernel,
        out_shape=[block] * 2,
        in_specs=[SM] + [ANY] * 6,
        out_specs=[VM] * 2,
        scratch_shapes=[pltpu.SemaphoreType.DMA((2, 2))],
        compiler_params=pltpu.CompilerParams(vmem_limit_bytes=SMALL_VMEM),
        cost_estimate=pl.CostEstimate(flops=0, transcendentals=0, bytes_accessed=1 << 20),
        name="ends",
    )(gids, g_l, ak_l, av_l, g_r, bk_r, bv_r)


def swap(value, bits):
    count = lax.axis_size(ALL)
    return lax.ppermute(value, ALL, [(i, i ^ bits) for i in range(count)])


def pick_slots(mask, a, b):
    return jnp.where(mask[:, None, None], a, b)


def masks_of(me, owners):
    differ = (me ^ owners) & 3
    rows = [differ == n for n in (1, 2, 3)]
    rows += [((me >> bit) & 1) == ((owners >> bit) & 1) for bit in (2, 3, 4, 5)]
    return jnp.stack(rows).astype(jnp.int32)


def spread(quarters, masks):
    value = quarters[0]
    given = [swap(quarters[n], n) for n in (1, 2, 3)]
    for n in (1, 2, 3):
        value = pick_slots(masks[n - 1] == 1, given[n - 1], value)
    for bit in (2, 3, 4, 5):
        value = pick_slots(masks[bit + 1] == 1, value, swap(value, 1 << bit))
    return [value] + [swap(value, n) for n in (1, 2, 3)]


def whole(queries, keys, values, global_ids, rand_pick):
    rows, width = queries.shape
    blocks = rows // BS
    count = lax.axis_size("blk")
    quarter = count // 4
    right = [(i, (i + quarter) % count) for i in range(count)]
    left = [(i, (i - quarter) % count) for i in range(count)]
    everyone = lax.axis_size(ALL)

    def to_right(v):
        return lax.ppermute(v, "blk", right)

    def to_left(v):
        return lax.ppermute(v, "blk", left)

    plane = everyone // 4

    def along(v, pairs):
        return lax.ppermute(
            v, ALL, [(p * plane + i, p * plane + j) for p in range(4) for i, j in pairs]
        )

    key_blocks = keys.reshape(blocks, BS, width)
    value_blocks = values.reshape(blocks, BS, width)
    (g,) = pack(global_ids, key_blocks, value_blocks, 0, G_N, joined=True)
    g_l, g_r = to_right(g), to_left(g)
    ak, av, tail, lead = pack(global_ids, key_blocks, value_blocks, G_N, A_N, ends=True)
    bk, bv = pack(global_ids, key_blocks, value_blocks, G_N + A_N, B_N)
    ak_l, av_l = to_right(ak), to_right(av)
    bk_r, bv_r = to_left(bk), to_left(bv)
    low = along(tail, [(i, i + 1) for i in range(plane - 1)])
    high = along(lead, [(i + 1, i) for i in range(plane - 1)])
    g_o = to_right(g_l)
    bk_l, bv_l = to_right(bk), to_right(bv)
    ak_r, av_r = to_left(ak), to_left(av)
    ak_o, bk_o = to_right(ak_l), to_left(bk_r)
    av_o, bv_o = to_right(av_l), to_left(bv_r)

    me = lax.axis_index(ALL)
    owners = global_ids // blocks
    distance = owners // plane - me // plane
    spot = me % plane
    edge = jnp.where(spot == 0, 0, jnp.where(spot == plane - 1, 1, 2))
    place = jnp.stack([me & 3, distance[0], distance[1], edge])
    place, masks = lax.optimization_barrier((place, masks_of(me, owners)))
    state = window(place, rand_pick, queries, keys, values, low, high)
    far_tail, far_lead = ends(global_ids, g_l, ak_l, av_l, g_r, bk_r, bv_r)
    first = along(far_tail, [(plane - 1, 0)])
    final = along(far_lead, [(0, plane - 1)])
    quarters = choose(global_ids, place, g, g_r, g_o, g_l)
    pieces = spread(quarters, masks)

    state = near(
        global_ids,
        rand_pick,
        place,
        queries,
        first,
        final,
        (g_r, ak_r, bk_r, av_r, bv_r),
        (g_l, ak_l, bk_l, av_l, bv_l),
        state,
    )
    weights, share, acc = score(
        global_ids, rand_pick, place, queries, pieces, (g_o, ak_o, bk_o), state
    )
    av_o = pltpu.with_memory_space_constraint(av_o, pltpu.VMEM)
    bv_o = pltpu.with_memory_space_constraint(bv_o, pltpu.VMEM)
    return last(global_ids, rand_pick, (g_o, av_o, bv_o), weights, share, acc, queries)


def solution(mesh):
    return jax.shard_map(
        whole,
        mesh=mesh,
        in_specs=(
            P(("blk", "sub"), None),
            P(("blk", "sub"), None),
            P(("blk", "sub"), None),
            P(),
            P(("blk", "sub"), None),
        ),
        out_specs=P(("blk", "sub"), None),
        check_vma=False,
    )
```

```python
import functools
import math

import jax
import jax.numpy as jnp
from jax import lax
from jax.experimental import pallas as pl
from jax.experimental.pallas import tpu as pltpu
from jax.sharding import PartitionSpec as P


H = 4
DH = 128
BS = 128
QB = 16
W = H * DH
SCALE_LOG2 = math.log2(math.e) / math.sqrt(DH)
G_N, A_N, B_N = 2, 6, 8
NEAR_VMEM, SCORE_VMEM, LAST_VMEM = 24 << 20, 24 << 20, 12 << 20
WINDOW_VMEM = 41 << 20
SMALL_VMEM = 8 << 20
HIDE = -1e30
ANY = pl.BlockSpec(memory_space=pl.ANY)
VM = pl.BlockSpec(memory_space=pltpu.VMEM)
SM = pl.BlockSpec(memory_space=pltpu.SMEM)
HB = pl.BlockSpec(memory_space=pltpu.HBM)


def first_two(gids, blocks):
    p0 = blocks - 1 - lax.rem(gids[0], blocks)
    p1 = blocks - 1 - lax.rem(gids[1], blocks)
    p1 = jnp.where(p1 == p0, lax.rem(p0 + 1, blocks), p1)
    return p0, p1, jnp.minimum(p0, p1), jnp.maximum(p0, p1)


def block_at(position, places, blocks):
    p0, p1, low, high = places
    if position == 0:
        return blocks - 1 - p0
    if position == 1:
        return blocks - 1 - p1
    k = position - 2
    k = k + (k >= low).astype(jnp.int32)
    return blocks - 1 - (k + (k >= high).astype(jnp.int32))


def position_of(block, places, blocks):
    p0, p1, low, high = places
    label = blocks - 1 - block
    rest = label - (label > low).astype(jnp.int32) - (label > high).astype(jnp.int32) + 2
    return jnp.where(label == p0, 0, jnp.where(label == p1, 1, rest))


def pack_kernel(start, count, joined, ends, gids, keys, values, *refs):
    blocks = keys.shape[0]
    places = first_two(gids, blocks)
    outs, (buf, in_sem, out_sem) = refs[:-3], refs[-3:]
    if joined:
        outs = (outs[0].at[0], outs[0].at[1])
    wanted = [block_at(start + i, places, blocks) for i in range(count)]
    if ends:
        wanted += [blocks - 1, 0]
    loads, stores = [], []
    for half, ref in enumerate((keys, values)):
        for i, block in enumerate(wanted):
            copy = pltpu.make_async_copy(ref.at[block], buf.at[half, i], in_sem.at[half, i])
            copy.start()
            loads.append((half, i, copy))
    for half, i, load in loads:
        load.wait()
        target = outs[half].at[i] if i < count else outs[2 + i - count].at[half]
        copy = pltpu.make_async_copy(buf.at[half, i], target, out_sem.at[half, i])
        copy.start()
        stores.append(copy)
    for copy in stores:
        copy.wait()


def pack(gids, keys, values, start, count, joined=False, ends=False):
    shapes = [jax.ShapeDtypeStruct((count, BS, W), keys.dtype)] * 2
    if joined:
        shapes = [jax.ShapeDtypeStruct((2, count, BS, W), keys.dtype)]
    if ends:
        shapes += [jax.ShapeDtypeStruct((2, BS, W), keys.dtype)] * 2
    places = count + 2 * ends
    return pl.pallas_call(
        functools.partial(pack_kernel, start, count, joined, ends),
        out_shape=shapes,
        in_specs=[SM, HB, HB],
        out_specs=[ANY] * len(shapes),
        scratch_shapes=[
            pltpu.VMEM((2, places, BS, W), keys.dtype),
            pltpu.SemaphoreType.DMA((2, places)),
            pltpu.SemaphoreType.DMA((2, places)),
        ],
        compiler_params=pltpu.CompilerParams(vmem_limit_bytes=56 << 20),
        cost_estimate=pl.CostEstimate(
            flops=0, transcendentals=0, bytes_accessed=places * 4 * BS * W * 2
        ),
        name="pack",
    )(gids, keys, values)


def dot_t(a, b):
    return lax.dot_general(a, b, (((1,), (1,)), ((), ())), preferred_element_type=jnp.float32)


def dot(a, b):
    return lax.dot_general(a, b, (((1,), (0,)), ((), ())), preferred_element_type=jnp.float32)


def head(h):
    return slice(h * DH, (h + 1) * DH)


def wide(column):
    return jnp.broadcast_to(column, (BS, DH))


def ones(rows):
    return jnp.ones((rows, DH), jnp.bfloat16)


def top_of(scores, old=None):
    tops = [jnp.max(s, axis=1, keepdims=True) for s in scores]
    top = wide(functools.reduce(jnp.maximum, tops))
    return top if old is None else jnp.maximum(top, old)


def weigh(s, top):
    parts = [
        jnp.exp2((s[:, n : n + DH] - top) * SCALE_LOG2) for n in range(0, s.shape[1], DH)
    ]
    return jnp.concatenate(parts, axis=1).astype(jnp.bfloat16)


def mix(w, v):
    return dot(w, jnp.concatenate([v, ones(v.shape[0])], axis=1))


def state_of(blocks):
    return [pltpu.VMEM((blocks, H, BS, DH), jnp.float32)] * 3


def fetch_pick(position, parts, dst, sem):
    at = 0
    for part in parts:
        count = part.shape[0]

        @pl.when((position >= at) & (position < at + count))
        def _(part=part, at=at, count=count):
            pltpu.make_async_copy(part.at[jnp.clip(position - at, 0, count - 1)], dst, sem).start()

        at += count


def window_kernel(blocks, place, picks, queries, keys, values, low, high, top_ref, total_ref, acc_ref, qbuf, kbuf, vbuf, sem):
    copies = [pltpu.make_async_copy(queries, qbuf, sem.at[0, 3])]
    for half, (ref, dst) in enumerate(((keys, kbuf), (values, vbuf))):
        copies.append(pltpu.make_async_copy(ref, dst.at[pl.ds(BS, blocks * BS)], sem.at[half, 0]))
        copies.append(pltpu.make_async_copy(low.at[half], dst.at[pl.ds(0, BS)], sem.at[half, 1]))
        copies.append(
            pltpu.make_async_copy(high.at[half], dst.at[pl.ds((blocks + 1) * BS, BS)], sem.at[half, 2])
        )
    for copy in copies:
        copy.start()
    for copy in copies:
        copy.wait()

    def step(j, carry):
        rows = pl.ds(pl.multiple_of(j * BS, BS), BS)
        span = pl.ds(pl.multiple_of(j * BS, BS), 3 * BS)
        no_low = jnp.where((place[3] == 0) & (j == 0), HIDE, 0.0)
        no_high = jnp.where((place[3] == 1) & (j == blocks - 1), HIDE, 0.0)
        q = [qbuf[rows, head(h)] for h in range(H)]
        k = [kbuf[span, head(h)] for h in range(H)]
        v = [vbuf[span, head(h)] for h in range(H)]
        scores = []
        for h in range(H):
            s = dot_t(q[h], k[h])
            scores.append(
                jnp.concatenate(
                    [s[:, :BS] + no_low, s[:, BS : 2 * BS], s[:, 2 * BS :] + no_high], axis=1
                )
            )
        tops = [top_of([scores[h]]) for h in range(H)]
        weights = [weigh(scores[h], tops[h]) for h in range(H)]
        mixed = [mix(weights[h], v[h]) for h in range(H)]
        for h in range(H):
            top_ref[j, h] = tops[h]
            total_ref[j, h] = mixed[h][:, DH:]
            acc_ref[j, h] = mixed[h][:, :DH]
        return carry

    lax.fori_loop(0, blocks, step, 0)


def window(place, picks, queries, keys, values, low, high):
    rows = queries.shape[0]
    blocks = rows // BS
    return pl.pallas_call(
        functools.partial(window_kernel, blocks),
        out_shape=state_of(blocks),
        in_specs=[SM, SM] + [ANY] * 5,
        out_specs=[VM] * 3,
        scratch_shapes=[
            pltpu.VMEM((rows, W), keys.dtype),
            pltpu.VMEM(((blocks + 2) * BS, W), keys.dtype),
            pltpu.VMEM(((blocks + 2) * BS, W), keys.dtype),
            pltpu.SemaphoreType.DMA((2, 4)),
        ],
        compiler_params=pltpu.CompilerParams(vmem_limit_bytes=WINDOW_VMEM),
        cost_estimate=pl.CostEstimate(
            flops=rows * 3 * BS * W * 4, transcendentals=rows * 3 * BS * H, bytes_accessed=20 << 20
        ),
        name="window",
    )(place, picks, queries, keys, values, low, high)


def near_kernel(blocks, gids, picks, place, queries, first, last, *refs):
    sides, refs = (refs[:5], refs[5:10]), refs[10:]
    top_in, total_in, acc_in, top_ref, total_ref, acc_ref, qbuf, wrap, buf, sem, pick_sem = refs
    places = first_two(gids, blocks)
    copies = [
        pltpu.make_async_copy(queries, qbuf, sem.at[0]),
        pltpu.make_async_copy(first, wrap.at[0], sem.at[1]),
        pltpu.make_async_copy(last, wrap.at[1], sem.at[2]),
    ]
    for copy in copies:
        copy.start()

    def fetch(j, carry):
        for side, column in ((0, 0), (1, 2)):
            g, a_k, b_k, a_v, b_v = sides[side]
            position = position_of(picks[j, column], places, blocks)
            fetch_pick(position, (g.at[0], a_k, b_k), buf.at[j, 0, side], pick_sem.at[j, 0, side])
            fetch_pick(position, (g.at[1], a_v, b_v), buf.at[j, 1, side], pick_sem.at[j, 1, side])
        return carry

    lax.fori_loop(0, blocks, fetch, 0)
    for copy in copies:
        copy.wait()

    def update(j, keys_of, values_of, source):
        rows = pl.ds(pl.multiple_of(j * BS, BS), BS)
        tops_in, totals_in, accs_in = source
        q = [qbuf[rows, head(h)] for h in range(H)]
        old_top = [tops_in[j, h] for h in range(H)]
        old_total = [totals_in[j, h] for h in range(H)]
        old_acc = [accs_in[j, h] for h in range(H)]
        scores = [dot_t(q[h], keys_of[h]) for h in range(H)]
        tops = [top_of([scores[h]], old_top[h]) for h in range(H)]
        weights = [weigh(scores[h], tops[h]) for h in range(H)]
        mixed = [mix(weights[h], values_of[h]) for h in range(H)]
        fades = [jnp.exp2((old_top[h] - tops[h]) * SCALE_LOG2) for h in range(H)]
        for h in range(H):
            top_ref[j, h] = tops[h]
            total_ref[j, h] = mixed[h][:, DH:] + fades[h] * old_total[h]
            acc_ref[j, h] = mixed[h][:, :DH] + fades[h] * old_acc[h]

    def step(j, carry):
        for half in range(2):
            for side in range(2):
                pltpu.make_async_copy(
                    sides[side][2].at[0], buf.at[j, half, side], pick_sem.at[j, half, side]
                ).wait()
        keys_of, values_of = [
            [
                jnp.concatenate([buf[j, half, side, :, head(h)] for side in range(2)], axis=0)
                for h in range(H)
            ]
            for half in range(2)
        ]
        update(j, keys_of, values_of, (top_in, total_in, acc_in))
        return carry

    lax.fori_loop(0, blocks, step, 0)

    @pl.when(place[3] < 2)
    def _():
        edge = jnp.where(place[3] == 0, 0, 1)
        update(
            jnp.where(place[3] == 0, 0, blocks - 1),
            [wrap[edge, 0, :, head(h)] for h in range(H)],
            [wrap[edge, 1, :, head(h)] for h in range(H)],
            (top_ref, total_ref, acc_ref),
        )


def near(gids, picks, place, queries, first, last, from_right, from_left, state):
    rows = queries.shape[0]
    blocks = rows // BS
    return pl.pallas_call(
        functools.partial(near_kernel, blocks),
        out_shape=state_of(blocks),
        in_specs=[SM, SM, SM] + [ANY] * 13 + [VM] * 3,
        out_specs=[VM] * 3,
        input_output_aliases={16: 0, 17: 1, 18: 2},
        scratch_shapes=[
            pltpu.VMEM((rows, W), queries.dtype),
            pltpu.VMEM((2, 2, BS, W), queries.dtype),
            pltpu.VMEM((blocks, 2, 2, BS, W), queries.dtype),
            pltpu.SemaphoreType.DMA((3,)),
            pltpu.SemaphoreType.DMA((blocks, 2, 2)),
        ],
        compiler_params=pltpu.CompilerParams(vmem_limit_bytes=NEAR_VMEM),
        cost_estimate=pl.CostEstimate(
            flops=rows * 2 * BS * W * 4, transcendentals=rows * 2 * BS * H, bytes_accessed=30 << 20
        ),
        name="near",
    )(gids, picks, place, queries, first, last, *from_right, *from_left, *state)


def score_kernel(blocks, gids, picks, place, q_ref, *refs):
    pieces, (g_o, ak_o, bk_o), refs = refs[:4], refs[4:7], refs[7:]
    top_in, total_in, acc_in, weight_ref, share_ref, acc_ref, shared, buf, shared_sem, sem = refs
    places = first_two(gids, blocks)
    copies = []
    for n, piece in enumerate(pieces):
        quarter = jnp.bitwise_and(jnp.bitwise_xor(place[0], n), 3)
        rows = piece.shape[1]
        start = jnp.bitwise_and(quarter, 1) * (2 * rows) + jnp.right_shift(quarter, 1) * rows
        at = pl.ds(pl.multiple_of(start, rows), rows)
        copies.append(pltpu.make_async_copy(piece, shared.at[:, at], shared_sem.at[n]))
    for copy in copies:
        copy.start()

    def fetch(j, carry):
        position = position_of(picks[j, 1], places, blocks)
        fetch_pick(position, (g_o.at[0], ak_o, bk_o), buf.at[j], sem.at[j])
        return carry

    lax.fori_loop(0, blocks, fetch, 0)
    for copy in copies:
        copy.wait()

    def step(j, carry):
        rows = pl.ds(pl.multiple_of(j * BS, BS), BS)
        pltpu.make_async_copy(bk_o.at[0], buf.at[j], sem.at[j]).wait()
        q = [q_ref[rows, head(h)] for h in range(H)]
        k = [
            jnp.concatenate(
                [shared[0, :BS, head(h)], shared[1, :BS, head(h)], buf[j, :, head(h)]], axis=0
            )
            for h in range(H)
        ]
        v = [jnp.concatenate([shared[n, BS:, head(h)] for n in range(2)], axis=0) for h in range(H)]
        old_top = [top_in[j, h] for h in range(H)]
        old_total = [total_in[j, h] for h in range(H)]
        old_acc = [acc_in[j, h] for h in range(H)]
        scores = [dot_t(q[h], k[h]) for h in range(H)]
        tops = [top_of([scores[h]], old_top[h]) for h in range(H)]
        weights = [weigh(scores[h], tops[h]) for h in range(H)]
        mixed = [mix(weights[h][:, : 2 * BS], v[h]) for h in range(H)]
        sums = [mixed[h][:, DH:] + dot(weights[h][:, 2 * BS :], ones(BS)) for h in range(H)]
        fades = [jnp.exp2((old_top[h] - tops[h]) * SCALE_LOG2) for h in range(H)]
        shares = [1.0 / (sums[h] + fades[h] * old_total[h]) for h in range(H)]
        for h in range(H):
            weight_ref[j, h] = weights[h][:, 2 * BS :]
            share_ref[j, h] = shares[h]
            acc_ref[j, h] = mixed[h][:, :DH] + old_acc[h] * fades[h]
        return carry

    lax.fori_loop(0, blocks, step, 0)


def score(gids, picks, place, queries, pieces, opposite, state):
    rows = queries.shape[0]
    blocks = rows // BS
    floats = jax.ShapeDtypeStruct((blocks, H, BS, DH), jnp.float32)
    return pl.pallas_call(
        functools.partial(score_kernel, blocks),
        out_shape=[jax.ShapeDtypeStruct((blocks, H, BS, BS), queries.dtype), floats, floats],
        in_specs=[SM, SM, SM, VM] + [ANY] * 7 + [VM] * 3,
        out_specs=[VM] * 3,
        input_output_aliases={12: 1, 13: 2},
        scratch_shapes=[
            pltpu.VMEM((2, 2 * BS, W), queries.dtype),
            pltpu.VMEM((blocks, BS, W), queries.dtype),
            pltpu.SemaphoreType.DMA((4,)),
            pltpu.SemaphoreType.DMA((blocks,)),
        ],
        compiler_params=pltpu.CompilerParams(vmem_limit_bytes=SCORE_VMEM),
        cost_estimate=pl.CostEstimate(
            flops=rows * BS * W * 10, transcendentals=rows * 3 * BS * H, bytes_accessed=28 << 20
        ),
        name="score",
    )(gids, picks, place, queries, *pieces, *opposite, *state)


def last_kernel(blocks, gids, picks, g, a_v, b_v, weights, share, acc, out, obuf, order, out_sem):
    places = first_two(gids, blocks)

    def store(j):
        rows = pl.ds(pl.multiple_of(j * BS, BS), BS)
        return pltpu.make_async_copy(obuf.at[j], out.at[rows], out_sem.at[j])

    def sort(j, counts):
        position = position_of(picks[j, 1], places, blocks)
        kind = (position >= G_N).astype(jnp.int32) + (position >= G_N + A_N).astype(jnp.int32)
        at = jnp.where(kind == 0, counts[0], jnp.where(kind == 1, counts[1], counts[2]))
        order[kind * blocks + at] = j
        return tuple(count + (kind == n).astype(jnp.int32) for n, count in enumerate(counts))

    zero = jnp.int32(0)
    counts = lax.fori_loop(0, blocks, sort, (zero, zero, zero))

    for kind, (values, begin) in enumerate(((g.at[1], 0), (a_v, G_N), (b_v, G_N + A_N))):
        count = counts[kind]

        def pair(n, carry, kind=kind, values=values, begin=begin, count=count):
            both = [
                order[kind * blocks + 2 * n],
                order[kind * blocks + jnp.minimum(2 * n + 1, count - 1)],
            ]
            mixed = []
            for j in both:
                at = position_of(picks[j, 1], places, blocks) - begin
                at = jnp.clip(at, 0, values.shape[0] - 1)
                mixed.append([dot(weights[j, h], values[at, :, head(h)]) for h in range(H)])
            done = [
                [((m + acc[j, h]) * share[j, h]).astype(obuf.dtype) for h, m in enumerate(ms)]
                for j, ms in zip(both, mixed)
            ]
            for j, parts in zip(both, done):
                for h in range(H):
                    obuf[j, :, head(h)] = parts[h]
            store(both[0]).start()

            @pl.when(both[1] != both[0])
            def _():
                store(both[1]).start()

            return carry

        lax.fori_loop(0, lax.div(count + 1, 2), pair, 0)

    def drain(j, carry):
        store(j).wait()
        return carry

    lax.fori_loop(0, blocks, drain, 0)


def last(gids, picks, parts, weights, share, acc, like):
    rows = like.shape[0]
    blocks = rows // BS
    return pl.pallas_call(
        functools.partial(last_kernel, blocks),
        out_shape=jax.ShapeDtypeStruct(like.shape, like.dtype),
        in_specs=[SM, SM] + [VM] * 6,
        out_specs=ANY,
        scratch_shapes=[
            pltpu.VMEM((blocks, BS, W), like.dtype),
            pltpu.SMEM((3 * blocks,), jnp.int32),
            pltpu.SemaphoreType.DMA((blocks,)),
        ],
        compiler_params=pltpu.CompilerParams(vmem_limit_bytes=LAST_VMEM),
        cost_estimate=pl.CostEstimate(
            flops=rows * BS * W * 2, transcendentals=0, bytes_accessed=10 << 20
        ),
        name="last",
    )(gids, picks, *parts, weights, share, acc)


ALL = ("blk", "sub")


def choose_kernel(gids, place, g, g_r, g_o, g_l, keep, give_1, give_2, give_3, sem):
    blocks = QB
    rows = keep.shape[1]
    p0, p1 = lax.rem(gids[0], blocks), lax.rem(gids[1], blocks)
    slots = (0, jnp.where(p0 == p1, 0, 1))
    outs = (keep, give_1, give_2, give_3)
    for i in range(2):
        distance = lax.rem(place[i + 1] + 4, 4)
        for d, source in enumerate((g, g_r, g_o, g_l)):

            @pl.when(distance == d)
            def _(i=i, source=source):
                for n, out in enumerate(outs):
                    quarter = jnp.bitwise_xor(place[0], n)
                    half = jnp.bitwise_and(quarter, 1)
                    at = pl.ds(pl.multiple_of(jnp.right_shift(quarter, 1) * rows, rows), rows)
                    pltpu.make_async_copy(source.at[half, slots[i], at], out.at[i], sem.at[i, n]).start()

    for i in range(2):
        for n, out in enumerate(outs):
            pltpu.make_async_copy(g.at[0, 0, pl.ds(0, rows)], out.at[i], sem.at[i, n]).wait()


def choose(gids, place, g, g_r, g_o, g_l):
    piece = jax.ShapeDtypeStruct((2, BS // 2, W), g.dtype)
    return pl.pallas_call(
        choose_kernel,
        out_shape=[piece] * 4,
        in_specs=[SM, SM] + [ANY] * 4,
        out_specs=[VM] * 4,
        scratch_shapes=[pltpu.SemaphoreType.DMA((2, 4))],
        compiler_params=pltpu.CompilerParams(vmem_limit_bytes=SMALL_VMEM),
        cost_estimate=pl.CostEstimate(flops=0, transcendentals=0, bytes_accessed=1 << 20),
        name="choose",
    )(gids, place, g, g_r, g_o, g_l)


def ends_kernel(gids, g_l, ak_l, av_l, g_r, bk_r, bv_r, tail, lead, sem):
    p0, p1, _, _ = first_two(gids, QB)
    cases = (
        (0, tail, g_l, (ak_l.at[0], av_l.at[0])),
        (QB - 1, lead, g_r, (bk_r.at[B_N - 1], bv_r.at[B_N - 1])),
    )
    for n, (label, out, g, rest) in enumerate(cases):
        for half in range(2):
            done = sem.at[n, half]

            @pl.when(p0 == label)
            def _(g=g, half=half, out=out, done=done):
                pltpu.make_async_copy(g.at[half, 0], out.at[half], done).start()

            @pl.when(p1 == label)
            def _(g=g, half=half, out=out, done=done):
                pltpu.make_async_copy(g.at[half, 1], out.at[half], done).start()

            @pl.when((p0 != label) & (p1 != label))
            def _(rest=rest, half=half, out=out, done=done):
                pltpu.make_async_copy(rest[half], out.at[half], done).start()

    for n, (_, out, _, rest) in enumerate(cases):
        for half in range(2):
            pltpu.make_async_copy(rest[half], out.at[half], sem.at[n, half]).wait()


def ends(gids, g_l, ak_l, av_l, g_r, bk_r, bv_r):
    block = jax.ShapeDtypeStruct((2, BS, W), g_l.dtype)
    return pl.pallas_call(
        ends_kernel,
        out_shape=[block] * 2,
        in_specs=[SM] + [ANY] * 6,
        out_specs=[VM] * 2,
        scratch_shapes=[pltpu.SemaphoreType.DMA((2, 2))],
        compiler_params=pltpu.CompilerParams(vmem_limit_bytes=SMALL_VMEM),
        cost_estimate=pl.CostEstimate(flops=0, transcendentals=0, bytes_accessed=1 << 20),
        name="ends",
    )(gids, g_l, ak_l, av_l, g_r, bk_r, bv_r)


def swap(value, bits):
    count = lax.axis_size(ALL)
    return lax.ppermute(value, ALL, [(i, i ^ bits) for i in range(count)])


def pick_slots(mask, a, b):
    return jnp.where(mask[:, None, None], a, b)


def masks_of(me, owners):
    differ = (me ^ owners) & 3
    rows = [differ == n for n in (1, 2, 3)]
    rows += [((me >> bit) & 1) == ((owners >> bit) & 1) for bit in (2, 3, 4, 5)]
    return jnp.stack(rows).astype(jnp.int32)


def spread(quarters, masks):
    value = quarters[0]
    given = [swap(quarters[n], n) for n in (1, 2, 3)]
    for n in (1, 2, 3):
        value = pick_slots(masks[n - 1] == 1, given[n - 1], value)
    for bit in (2, 3, 4, 5):
        value = pick_slots(masks[bit + 1] == 1, value, swap(value, 1 << bit))
    return [value] + [swap(value, n) for n in (1, 2, 3)]


def whole(queries, keys, values, global_ids, rand_pick):
    rows, width = queries.shape
    blocks = rows // BS
    count = lax.axis_size("blk")
    quarter = count // 4
    right = [(i, (i + quarter) % count) for i in range(count)]
    left = [(i, (i - quarter) % count) for i in range(count)]
    everyone = lax.axis_size(ALL)

    def to_right(v):
        return lax.ppermute(v, "blk", right)

    def to_left(v):
        return lax.ppermute(v, "blk", left)

    plane = everyone // 4

    def along(v, pairs):
        return lax.ppermute(
            v, ALL, [(p * plane + i, p * plane + j) for p in range(4) for i, j in pairs]
        )

    key_blocks = keys.reshape(blocks, BS, width)
    value_blocks = values.reshape(blocks, BS, width)
    (g,) = pack(global_ids, key_blocks, value_blocks, 0, G_N, joined=True)
    g_l, g_r = to_right(g), to_left(g)
    ak, av, tail, lead = pack(global_ids, key_blocks, value_blocks, G_N, A_N, ends=True)
    bk, bv = pack(global_ids, key_blocks, value_blocks, G_N + A_N, B_N)
    ak_l, av_l = to_right(ak), to_right(av)
    bk_r, bv_r = to_left(bk), to_left(bv)
    low = along(tail, [(i, i + 1) for i in range(plane - 1)])
    high = along(lead, [(i + 1, i) for i in range(plane - 1)])
    g_o = to_right(g_l)
    bk_l, bv_l = to_right(bk), to_right(bv)
    ak_r, av_r = to_left(ak), to_left(av)
    ak_o, bk_o = to_right(ak_l), to_left(bk_r)
    av_o, bv_o = to_right(av_l), to_left(bv_r)

    me = lax.axis_index(ALL)
    owners = global_ids // blocks
    distance = owners // plane - me // plane
    spot = me % plane
    edge = jnp.where(spot == 0, 0, jnp.where(spot == plane - 1, 1, 2))
    place = jnp.stack([me & 3, distance[0], distance[1], edge])
    place, masks = lax.optimization_barrier((place, masks_of(me, owners)))
    state = window(place, rand_pick, queries, keys, values, low, high)
    far_tail, far_lead = ends(global_ids, g_l, ak_l, av_l, g_r, bk_r, bv_r)
    first = along(far_tail, [(plane - 1, 0)])
    final = along(far_lead, [(0, plane - 1)])
    quarters = choose(global_ids, place, g, g_r, g_o, g_l)
    pieces = spread(quarters, masks)

    state = near(
        global_ids,
        rand_pick,
        place,
        queries,
        first,
        final,
        (g_r, ak_r, bk_r, av_r, bv_r),
        (g_l, ak_l, bk_l, av_l, bv_l),
        state,
    )
    weights, share, acc = score(
        global_ids, rand_pick, place, queries, pieces, (g_o, ak_o, bk_o), state
    )
    av_o = pltpu.with_memory_space_constraint(av_o, pltpu.VMEM)
    bv_o = pltpu.with_memory_space_constraint(bv_o, pltpu.VMEM)
    return last(global_ids, rand_pick, (g_o, av_o, bv_o), weights, share, acc, queries)


def solution(mesh):
    return jax.shard_map(
        whole,
        mesh=mesh,
        in_specs=(
            P(("blk", "sub"), None),
            P(("blk", "sub"), None),
            P(("blk", "sub"), None),
            P(),
            P(("blk", "sub"), None),
        ),
        out_specs=P(("blk", "sub"), None),
        check_vma=False,
    )
```
